32 devices in a mesh: gx: 16 (over z, y, core), gy: 2 (over x).
Axes of the slice: x: 2, y: 2, z: 4, core: 2. Of those that a mesh axis runs over, the one named last changes fastest.
Arguments:
- velocity: float32 [3, 64, 32, 128], P(None, 'gx', 'gy'), may hold values from -3 to 3
- cauchy_green: float32 [6, 64, 32, 128], P(None, 'gx', 'gy'), may hold values from -0.25 to 1.5, as said below
- labels: int32 [64, 32, 128], P('gx', 'gy'), may hold values from 0 to 4
Outputs:
- new_velocity: float32 [3, 64, 32, 128], P(None, 'gx', 'gy')
- new_cauchy_green: float32 [6, 64, 32, 128], P(None, 'gx', 'gy')
- new_fraction: float32 [64, 32, 128], P('gx', 'gy')
The draws below stay inside these ranges and needn't reach their ends.
Inputs may be any that keep to these rules, and one draw needn't show every extreme that they name: `cauchy_green`: the six components are xx, yy, zz, xy, xz, yz of a symmetric tensor; the three diagonal ones lie in 0.6 to 1.5 and the off-diagonal ones in -0.25 to 0.25.
All inputs are finite; a program needn't handle non-finite values.
Results may differ from the reference program's by a relative error of at most 0.0003.
Values sent between devices are 32-bit elements; how exact they have to be, the bound alone decides.
A program may use at most 64 MiB of HBM per device.

```python
import math
import jax
import jax.numpy as jnp
from jax import lax

NZ = 128
NX = 64
NY = 32


def draw_cauchy_green(key, part):
    key_diagonal = jax.random.fold_in(key, 11)
    key_off = jax.random.fold_in(key, 12)
    diagonal_part = jax.random.uniform(key_diagonal, (3, NX, NY, NZ), jnp.float32, 0.7, 1.3)
    off_part = jax.random.uniform(key_off, (3, NX, NY, NZ), jnp.float32, -0.2, 0.2)
    return jnp.concatenate([diagonal_part, off_part], 0)


def place_ends(array, rng, least, high):
    shape = array.shape
    spot = [jax.random.randint(jax.random.fold_in(rng, axis), (), 0, shape[axis]) for axis in range(len(shape))]
    array = array.at[tuple(spot)].set(least)
    longest = shape.index(max(shape))
    spot[longest] = (spot[longest] + 1) % shape[longest]
    return array.at[tuple(spot)].set(high)


def steps_of(rng, extent, pieces, smallest, largest):
    def one(dim, parts):
        draws = jax.random.uniform(jax.random.fold_in(jax.random.fold_in(rng, 6), dim), (parts,), jnp.float32, smallest / len(pieces), largest / len(pieces))
        return jnp.repeat(jnp.exp(draws), extent[dim] // parts).reshape((-1,) + (1,) * (len(extent) - dim - 1))

    level = one(*pieces[0])
    for cut in pieces[1:]:
        level = level * one(*cut)
    return level


def centred(own_key, dims, deviation, bound, shards=(), kind=jnp.bfloat16):
    values = jax.random.normal(own_key, dims, jnp.float32) * deviation
    if len(shards) > 0:
        values = steps_of(own_key, dims, shards, -0.22, 0.18) * values
    return jnp.clip(values, min=-bound, max=bound).astype(kind)


def setup_inputs(seed: int = 0) -> dict:
    splits = jax.random.split(jax.random.key(seed), 4)
    return {
        "velocity": centred(splits[0], (3, NX, NY, NZ), 0.5, 3.0, ((1, 16), (2, 2)), jnp.float32),
        "cauchy_green": draw_cauchy_green(jax.random.fold_in(splits[3], 71), 0),
        "labels": place_ends(jax.random.randint(splits[2], (NX, NY, NZ), 0, 5), jax.random.fold_in(splits[2], 1), 0, 4).astype(jnp.int32),
    }


time_step = 0.1
shear_modulus = 4.0
dilation = 0.5
weno_eps = 1e-6
pair_list = ((0, 0), (1, 1), (2, 2), (0, 1), (0, 2), (1, 2))
slot_table = ((0, 3, 4), (3, 1, 5), (4, 5, 2))


def weno_face(minus_two, minus_one, center, plus_one, plus_two):
    poly_zero = (2.0 * minus_two - 7.0 * minus_one + 11.0 * center) / 6.0
    poly_one = (-minus_one + 5.0 * center + 2.0 * plus_one) / 6.0
    poly_two = (2.0 * center + 5.0 * plus_one - plus_two) / 6.0
    curve_zero = minus_two - 2.0 * minus_one + center
    slope_zero = minus_two - 4.0 * minus_one + 3.0 * center
    curve_one = minus_one - 2.0 * center + plus_one
    slope_one = minus_one - plus_one
    curve_two = center - 2.0 * plus_one + plus_two
    slope_two = 3.0 * center - 4.0 * plus_one + plus_two
    smooth_zero = weno_eps + 13.0 / 12.0 * curve_zero * curve_zero + 0.25 * slope_zero * slope_zero
    smooth_one = weno_eps + 13.0 / 12.0 * curve_one * curve_one + 0.25 * slope_one * slope_one
    smooth_two = weno_eps + 13.0 / 12.0 * curve_two * curve_two + 0.25 * slope_two * slope_two
    weight_zero = 0.1 / (smooth_zero * smooth_zero)
    weight_one = 0.6 / (smooth_one * smooth_one)
    weight_two = 0.3 / (smooth_two * smooth_two)
    return (weight_zero * poly_zero + weight_one * poly_one + weight_two * poly_two) / (weight_zero + weight_one + weight_two)


def face_flux(shifted, speed_face):
    upwind_left = weno_face(shifted(-2), shifted(-1), shifted(0), shifted(1), shifted(2))
    upwind_right = weno_face(shifted(3), shifted(2), shifted(1), shifted(0), shifted(-1))
    return speed_face * jnp.where(speed_face >= 0.0, upwind_left, upwind_right)


def transport_field(quantity, velocity):
    summed = jnp.zeros_like(quantity)
    for direction in range(3):
        advecting = velocity[direction]
        speed_face = 0.5 * (advecting + jnp.roll(advecting, -1, direction))

        def shifted(offset, direction=direction):
            return jnp.roll(quantity, -offset, direction)

        flux_face = face_flux(shifted, speed_face)
        summed = summed + quantity * (speed_face - jnp.roll(speed_face, 1, direction)) - (flux_face - jnp.roll(flux_face, 1, direction))
    return summed


def central(quantity, direction):
    return 0.5 * (jnp.roll(quantity, -1, direction) - jnp.roll(quantity, 1, direction))


def advance(green, fraction, transported, gradient):
    updated = []
    for component in range(6):
        left_index, right_index = pair_list[component]
        stretch = jnp.zeros_like(green[0])
        for inner_index in range(3):
            stretch = stretch + gradient[left_index][inner_index] * green[slot_table[inner_index][right_index]]
            stretch = stretch + green[slot_table[left_index][inner_index]] * gradient[right_index][inner_index]
        updated.append(green[component] + time_step * (transported[component] + stretch))
    return jnp.stack(updated), fraction + time_step * transported[6]


def membrane_stress(green, fraction):
    determinant = (green[0] * (green[1] * green[2] - green[5] * green[5])
                   - green[3] * (green[3] * green[2] - green[5] * green[4])
                   + green[4] * (green[3] * green[5] - green[1] * green[4]))
    dilate = dilation * (determinant - 1.0)
    stress_parts = []
    for component in range(6):
        if component < 3:
            stress_parts.append(green[component] - 1.0 + dilate)
        else:
            stress_parts.append(green[component])
    return shear_modulus * fraction * jnp.stack(stress_parts)


def sine_numbers(length):
    wave_index = jnp.arange(length, dtype=jnp.int32)
    silent = wave_index % (length // 2) == 0
    sine_value = jnp.sin((2.0 * math.pi / length) * wave_index.astype(jnp.float32))
    return jnp.where(silent, 0.0, sine_value).astype(jnp.float32), silent


def reference(velocity, cauchy_green, labels):
    fraction = labels.astype(jnp.float32) * 0.25
    carried = jnp.concatenate([cauchy_green, fraction[None]], 0)
    transported = lax.map(lambda quantity: transport_field(quantity, velocity), carried)
    gradient = [[central(velocity[left_index], right_index) for right_index in range(3)] for left_index in range(3)]
    new_green, new_fraction = advance(cauchy_green, fraction, transported, gradient)
    stress = membrane_stress(new_green, new_fraction)
    force = jnp.stack([central(stress[slot_table[left_index][0]], 0) + central(stress[slot_table[left_index][1]], 1)
                       + central(stress[slot_table[left_index][2]], 2) for left_index in range(3)])
    predicted = velocity + time_step * force
    spectrum = jnp.fft.fftn(predicted, axes=(1, 2, 3))
    sine_x, silent_x = sine_numbers(NX)
    sine_y, silent_y = sine_numbers(NY)
    sine_z, silent_z = sine_numbers(NZ)
    live_mode = jnp.logical_not(silent_x[:, None, None] & silent_y[None, :, None] & silent_z[None, None, :])
    sine_list = (sine_x[:, None, None], sine_y[None, :, None], sine_z[None, None, :])
    norm_sq = sine_list[0] * sine_list[0] + sine_list[1] * sine_list[1] + sine_list[2] * sine_list[2]
    inner_sum = sine_list[0] * spectrum[0] + sine_list[1] * spectrum[1] + sine_list[2] * spectrum[2]
    ratio = jnp.where(live_mode, inner_sum / jnp.where(live_mode, norm_sq, 1.0), 0.0)
    projected = jnp.stack([spectrum[index_c] - sine_list[index_c] * ratio for index_c in range(3)])
    new_velocity = jnp.real(jnp.fft.ifftn(projected, axes=(1, 2, 3))).astype(jnp.float32)
    return new_velocity, new_green, new_fraction
```

```python
import functools
import math

import jax
import jax.numpy as jnp
import numpy as np
from jax import lax
from jax.experimental import pallas as pl
from jax.experimental.pallas import tpu as pltpu
from jax.sharding import PartitionSpec as P

time_step = 0.1
shear_modulus = 4.0
dilation = 0.5
weno_eps = 1e-06
pair_list = ((0, 0), (1, 1), (2, 2), (0, 1), (0, 2), (1, 2))
slot_table = ((0, 3, 4), (3, 1, 5), (4, 5, 2))


def padded_2(block, sides, width):
    for axis, dim in sides:
        count = lax.axis_size(axis)
        forward = [(i, i + 1) for i in range(count - 1)]
        forward.append((count - 1, 0))
        backward = [(target, source) for source, target in forward]
        low = lax.ppermute(
            lax.slice_in_dim(block, block.shape[dim] - width, None, axis=dim), axis, forward
        )
        high = lax.ppermute(lax.slice_in_dim(block, 0, width, axis=dim), axis, backward)
        block = jnp.concatenate([low, block, high], axis=dim)
    return block


def weno_face(minus_two, minus_one, center, plus_one, plus_two):
    poly_zero = (2.0 * minus_two - 7.0 * minus_one + 11.0 * center) / 6.0
    poly_one = (-minus_one + 5.0 * center + 2.0 * plus_one) / 6.0
    poly_two = (2.0 * center + 5.0 * plus_one - plus_two) / 6.0
    curve_zero = minus_two - 2.0 * minus_one + center
    slope_zero = minus_two - 4.0 * minus_one + 3.0 * center
    curve_one = minus_one - 2.0 * center + plus_one
    slope_one = minus_one - plus_one
    curve_two = center - 2.0 * plus_one + plus_two
    slope_two = 3.0 * center - 4.0 * plus_one + plus_two
    smooth_zero = weno_eps + 13.0 / 12.0 * curve_zero * curve_zero + 0.25 * slope_zero * slope_zero
    smooth_one = weno_eps + 13.0 / 12.0 * curve_one * curve_one + 0.25 * slope_one * slope_one
    smooth_two = weno_eps + 13.0 / 12.0 * curve_two * curve_two + 0.25 * slope_two * slope_two
    weight_zero = 0.1 / (smooth_zero * smooth_zero)
    weight_one = 0.6 / (smooth_one * smooth_one)
    weight_two = 0.3 / (smooth_two * smooth_two)
    return (weight_zero * poly_zero + weight_one * poly_one + weight_two * poly_two) / (
        weight_zero + weight_one + weight_two
    )


def face_flux(shifted, speed_face):
    upwind_left = weno_face(shifted(-2), shifted(-1), shifted(0), shifted(1), shifted(2))
    upwind_right = weno_face(shifted(3), shifted(2), shifted(1), shifted(0), shifted(-1))
    return speed_face * jnp.where(speed_face >= 0.0, upwind_left, upwind_right)


def sweep(quantity, advecting, sweep_dim, anchor, count):

    def shifted(offset):
        return lax.slice_in_dim(
            quantity, anchor - 1 + offset, anchor + offset + count, axis=sweep_dim
        )

    speed_face = 0.5 * (
        lax.slice_in_dim(advecting, anchor - 1, anchor + count, axis=sweep_dim - 1)
        + lax.slice_in_dim(advecting, anchor, anchor + count + 1, axis=sweep_dim - 1)
    )
    flux_face = face_flux(shifted, speed_face)
    flux_upper = lax.slice_in_dim(flux_face, 1, count + 1, axis=sweep_dim)
    flux_lower = lax.slice_in_dim(flux_face, 0, count, axis=sweep_dim)
    center = lax.slice_in_dim(quantity, anchor, anchor + count, axis=sweep_dim)
    spread = lax.slice_in_dim(speed_face, 1, count + 1, axis=sweep_dim - 1) - lax.slice_in_dim(
        speed_face, 0, count, axis=sweep_dim - 1
    )
    return center * spread - (flux_upper - flux_lower)


def sweep_periodic(quantity, advecting):

    def shifted(offset):
        return jnp.roll(quantity, -offset, 3)

    speed_face = 0.5 * (advecting + jnp.roll(advecting, -1, 2))
    flux_face = face_flux(shifted, speed_face)
    return quantity * (speed_face - jnp.roll(speed_face, 1, 2)) - (
        flux_face - jnp.roll(flux_face, 1, 3)
    )


def region_gradient(padded, anchor, count_x, count_y):
    gradient = []
    for component in range(3):
        advecting = padded[7 + component]
        center = advecting[anchor : anchor + count_x, anchor : anchor + count_y]
        along_x = 0.5 * (
            advecting[anchor + 1 : anchor + 1 + count_x, anchor : anchor + count_y]
            - advecting[anchor - 1 : anchor - 1 + count_x, anchor : anchor + count_y]
        )
        along_y = 0.5 * (
            advecting[anchor : anchor + count_x, anchor + 1 : anchor + 1 + count_y]
            - advecting[anchor : anchor + count_x, anchor - 1 : anchor - 1 + count_y]
        )
        along_z = 0.5 * (jnp.roll(center, -1, 2) - jnp.roll(center, 1, 2))
        gradient.append([along_x, along_y, along_z])
    return gradient


def advance(green, fraction, transported, gradient):
    updated = []
    for component in range(6):
        left_index, right_index = pair_list[component]
        stretch = jnp.zeros_like(green[0])
        for inner_index in range(3):
            stretch = (
                stretch
                + gradient[left_index][inner_index] * green[slot_table[inner_index][right_index]]
            )
            stretch = (
                stretch
                + green[slot_table[left_index][inner_index]] * gradient[right_index][inner_index]
            )
        updated.append(green[component] + time_step * (transported[component] + stretch))
    return (jnp.stack(updated), fraction + time_step * transported[6])


def membrane_stress(green, fraction):
    determinant = (
        green[0] * (green[1] * green[2] - green[5] * green[5])
        - green[3] * (green[3] * green[2] - green[5] * green[4])
        + green[4] * (green[3] * green[5] - green[1] * green[4])
    )
    dilate = dilation * (determinant - 1.0)
    stress_parts = []
    for component in range(6):
        if component < 3:
            stress_parts.append(green[component] - 1.0 + dilate)
        else:
            stress_parts.append(green[component])
    return shear_modulus * fraction * jnp.stack(stress_parts)


def update_region(padded, anchor, count_x, count_y):
    carried = padded[:7]
    transported = sweep(
        carried[:, :, anchor : anchor + count_y],
        padded[7, :, anchor : anchor + count_y],
        1,
        anchor,
        count_x,
    )
    transported = transported + sweep(
        carried[:, anchor : anchor + count_x],
        padded[8, anchor : anchor + count_x],
        2,
        anchor,
        count_y,
    )
    region = padded[:, anchor : anchor + count_x, anchor : anchor + count_y]
    transported = transported + sweep_periodic(region[:7], region[9])
    gradient = region_gradient(padded, anchor, count_x, count_y)
    new_green, new_fraction = advance(region[:6], region[6], transported, gradient)
    return (new_green, new_fraction, membrane_stress(new_green, new_fraction))


def derive_x(widened):
    return 0.5 * (widened[..., 2:, 1:-1, :] - widened[..., :-2, 1:-1, :])


def derive_y(widened):
    return 0.5 * (widened[..., 1:-1, 2:, :] - widened[..., 1:-1, :-2, :])


def derive_z(widened):
    inside = widened[..., 1:-1, 1:-1, :]
    return 0.5 * (jnp.roll(inside, -1, -1) - jnp.roll(inside, 1, -1))


def stress_force(widened):
    return jnp.stack(
        [
            derive_x(widened[slot_table[index_row][0]])
            + derive_y(widened[slot_table[index_row][1]])
            + derive_z(widened[slot_table[index_row][2]])
            for index_row in range(3)
        ]
    )


def dft_tables(length):
    wave_index = jnp.arange(length, dtype=jnp.int32)
    phase_index = wave_index[:, None] * wave_index[None, :] % length
    angle_table = 2.0 * math.pi / length * phase_index.astype(jnp.float32)
    return (jnp.cos(angle_table), jnp.sin(angle_table))


def contract(einsum_form, values, dft_table):
    return jnp.einsum(einsum_form, values, dft_table, precision=lax.Precision.HIGHEST)


def forward_transform(cell_field):
    components, cells_x, cells_y, length_z = cell_field.shape
    length_x = cells_x * lax.axis_size("gx")
    length_y = cells_y * lax.axis_size("gy")
    slab_z = length_z // lax.axis_size("gx")
    cosine_z, sine_z = dft_tables(length_z)
    real_z = contract("cxyz,zk->cxyk", cell_field, cosine_z)
    imag_z = -contract("cxyz,zk->cxyk", cell_field, sine_z)
    lines_x = lax.all_to_all(
        jnp.stack([real_z, imag_z], 1), "gx", split_axis=4, concat_axis=2, tiled=True
    )
    lines_x = lines_x.reshape(components, 2, length_x, cells_y * slab_z)
    cosine_x, sine_x = dft_tables(length_x)
    real_part = lines_x[:, 0]
    imag_part = lines_x[:, 1]
    real_x = contract("cxm,xk->ckm", real_part, cosine_x) + contract(
        "cxm,xk->ckm", imag_part, sine_x
    )
    imag_x = contract("cxm,xk->ckm", imag_part, cosine_x) - contract(
        "cxm,xk->ckm", real_part, sine_x
    )
    paired_x = jnp.stack([real_x, imag_x], 1).reshape(components, 2, length_x, cells_y, slab_z)
    lines_y = lax.all_to_all(paired_x, "gy", split_axis=2, concat_axis=3, tiled=True)
    cosine_y, sine_y = dft_tables(length_y)
    real_part = lines_y[:, 0]
    imag_part = lines_y[:, 1]
    real_y = contract("cayz,yk->ckaz", real_part, cosine_y) + contract(
        "cayz,yk->ckaz", imag_part, sine_y
    )
    imag_y = contract("cayz,yk->ckaz", imag_part, cosine_y) - contract(
        "cayz,yk->ckaz", real_part, sine_y
    )
    return (real_y, imag_y)


def inverse_transform(real_k, imag_k, cells_y, length_z):
    components, length_y, block_x, slab_z = real_k.shape
    length_x = block_x * lax.axis_size("gy")
    cosine_y, sine_y = dft_tables(length_y)
    real_y = contract("ckaz,ky->cayz", real_k, cosine_y) - contract("ckaz,ky->cayz", imag_k, sine_y)
    imag_y = contract("ckaz,ky->cayz", real_k, sine_y) + contract("ckaz,ky->cayz", imag_k, cosine_y)
    lines_x = lax.all_to_all(
        jnp.stack([real_y, imag_y], 1), "gy", split_axis=3, concat_axis=2, tiled=True
    )
    lines_x = lines_x.reshape(components, 2, length_x, cells_y * slab_z)
    cosine_x, sine_x = dft_tables(length_x)
    real_part = lines_x[:, 0]
    imag_part = lines_x[:, 1]
    real_x = contract("ckm,kx->cxm", real_part, cosine_x) - contract(
        "ckm,kx->cxm", imag_part, sine_x
    )
    imag_x = contract("ckm,kx->cxm", real_part, sine_x) + contract(
        "ckm,kx->cxm", imag_part, cosine_x
    )
    paired_x = jnp.stack([real_x, imag_x], 1).reshape(components, 2, length_x, cells_y, slab_z)
    slab_pairs = lax.all_to_all(paired_x, "gx", split_axis=2, concat_axis=4, tiled=True)
    cosine_z, sine_z = dft_tables(length_z)
    result = contract("cxyk,kz->cxyz", slab_pairs[:, 0], cosine_z) - contract(
        "cxyk,kz->cxyz", slab_pairs[:, 1], sine_z
    )
    return result / float(length_x * length_y * length_z)


def sine_numbers(wave_index, length):
    silent = wave_index % (length // 2) == 0
    sine_value = jnp.sin(2.0 * math.pi / length * wave_index.astype(jnp.float32))
    return (jnp.where(silent, 0.0, sine_value), silent)


def wave_numbers(length_y, block_x, slab_z, length_x, length_z):
    index_y = jnp.arange(length_y, dtype=jnp.int32)
    index_x = lax.axis_index("gy") * block_x + jnp.arange(block_x, dtype=jnp.int32)
    index_z = lax.axis_index("gx") * slab_z + jnp.arange(slab_z, dtype=jnp.int32)
    sine_x, silent_x = sine_numbers(index_x, length_x)
    sine_y, silent_y = sine_numbers(index_y, length_y)
    sine_z, silent_z = sine_numbers(index_z, length_z)
    live_mode = jnp.logical_not(
        silent_y[:, None, None] & silent_x[None, :, None] & silent_z[None, None, :]
    )
    return ((sine_x[None, :, None], sine_y[:, None, None], sine_z[None, None, :]), live_mode)


def local(velocity, cauchy_green, labels):
    cells_x = velocity.shape[1]
    cells_y = velocity.shape[2]
    length_z = velocity.shape[3]
    fraction = labels.astype(jnp.float32) * 0.25
    stacked = jnp.concatenate([cauchy_green, fraction[None], velocity], 0)
    padded = padded_2(stacked, (("gx", 1), ("gy", 2)), 4)
    green_wide, fraction_wide, stress_wide = update_region(padded, 3, cells_x + 2, cells_y + 2)
    new_green = green_wide[:, 1:-1, 1:-1]
    new_fraction = fraction_wide[1:-1, 1:-1]
    predicted = velocity + time_step * stress_force(stress_wide)
    length_x = cells_x * lax.axis_size("gx")
    velocity_wide = padded_2(predicted, (("gx", 1), ("gy", 2)), 1)
    divergence = (
        derive_x(velocity_wide[0]) + derive_y(velocity_wide[1]) + derive_z(velocity_wide[2])
    )
    real_k, imag_k = forward_transform(divergence[None])
    sine_list, live_mode = wave_numbers(
        real_k.shape[1], real_k.shape[2], real_k.shape[3], length_x, length_z
    )
    norm_sq = (
        sine_list[0] * sine_list[0] + sine_list[1] * sine_list[1] + sine_list[2] * sine_list[2]
    )
    safe_norm = jnp.where(live_mode, norm_sq, 1.0)
    pressure_real = jnp.where(live_mode, -real_k[0] / safe_norm, 0.0)
    pressure_imag = jnp.where(live_mode, -imag_k[0] / safe_norm, 0.0)
    pressure = inverse_transform(pressure_real[None], pressure_imag[None], cells_y, length_z)
    pressure_wide = padded_2(pressure, (("gx", 1), ("gy", 2)), 1)
    new_velocity = predicted - jnp.stack(
        [derive_x(pressure_wide[0]), derive_y(pressure_wide[0]), derive_z(pressure_wide[0])]
    )
    return (new_velocity, new_green, new_fraction)


def hartley(length):
    index = np.arange(length)
    angle = 2.0 * np.pi / length * (np.outer(index, index) % length)
    return np.cos(angle) + np.sin(angle)


def sine_squares(length):
    index = np.arange(length)
    sine = np.where(index % (length // 2) == 0, 0.0, np.sin(2.0 * np.pi / length * index))
    return sine * sine


def split_table(table):
    high = np.asarray(table, jnp.bfloat16)
    low = np.asarray(table - np.asarray(high, np.float64), jnp.bfloat16)
    return np.stack([high, low])


def back_lanes(cells_x, cells_y):
    return -(-(cells_x + 2) * (cells_y + 2) // 128) * 128


def spectral_tables(count_x, count_y, cells_x, cells_y, length_z):
    length_x, length_y = count_x * cells_x, count_y * cells_y
    devices = count_x * count_y
    rows = length_z // devices
    table_x, table_y, table_z = hartley(length_x), hartley(length_y), hartley(length_z)
    wide = cells_x + 4
    stencils = (
        {0: 1.0},
        {-1: 0.5, 1: -0.5},
        {-2: 0.25, 0: -0.5, 2: 0.25},
    )
    field_orders = ((2, 0), (1, 1), (1, 0), (0, 2), (0, 1), (0, 0))
    send_table = np.zeros((count_y, 6, cells_x, cells_y, wide, length_y))
    near_x, near_y = cells_x + 2, cells_y + 2
    take_table = np.zeros((3, cells_x, cells_y, back_lanes(cells_x, cells_y)))
    turn_table = np.zeros((length_y, count_y, near_y))
    for block in range(count_y):
        place = block * cells_y + np.arange(cells_y)
        along = [
            sum(w * table_y[(place + o) % length_y] for o, w in stencil.items())
            for stencil in stencils
        ]
        for field, (order_x, order_y) in enumerate(field_orders):
            for cell in range(cells_x):
                for offset, weight in stencils[order_x].items():
                    send_table[block, field, cell, :, cell + 2 + offset] += weight * along[order_y]
        ring = (block * cells_y + np.arange(near_y) - 1) % length_y
        turn_table[:, block] = table_y[:, ring]
    for x in range(cells_x):
        for y in range(cells_y):
            place = (x + 1) * near_y + y + 1
            take_table[0, x, y, place + near_y] = 0.5
            take_table[0, x, y, place - near_y] = -0.5
            take_table[1, x, y, place + 1] = 0.5
            take_table[1, x, y, place - 1] = -0.5
            take_table[2, x, y, place] = 1.0
    same = np.eye(rows)
    reach = (
        np.arange(count_x)[None, :] * cells_x + np.arange(wide)[:, None] - 2
    ) % length_x
    solve_in = np.einsum("kib,qr->kqibr", table_x[:, reach], same).reshape(
        length_x * rows, wide * count_x * rows
    )
    home = np.arange(count_x)[None, :] * cells_x + np.arange(near_x)[:, None] - 1
    solve_out = np.einsum("ibk,qr->ibqkr", table_x[home % length_x], same).reshape(
        near_x * count_x * rows, length_x * rows
    )
    square_xy = np.repeat(sine_squares(length_x), rows)[:, None] + sine_squares(length_y)[None, :]
    square_z = sine_squares(length_z).reshape(devices, rows)
    square_z = np.tile(square_z, (1, 8 // rows))[:, :, None] * np.ones((1, 1, length_y))
    send_table = send_table.reshape(count_y, 6 * cells_x * cells_y, wide * length_y)
    take_table = take_table.reshape(3 * cells_x * cells_y, -1)
    return (
        split_table(table_z),
        np.moveaxis(split_table(send_table), 0, 1),
        split_table(solve_in),
        split_table(solve_out),
        np.asarray(square_xy.reshape(-1, 8, length_y), np.float32),
        np.asarray(square_z, np.float32),
        np.asarray(take_table, jnp.bfloat16),
        split_table(turn_table.reshape(length_y, count_y * near_y)),
    )


def shift(values, offset, axis):
    extent = values.shape[axis]
    if offset % extent == 0:
        return values
    return pltpu.roll(values, (-offset) % extent, axis)


def weno_one(a, b, c, d, e):
    poly_zero = 2.0 * a - 7.0 * b + 11.0 * c
    poly_one = 5.0 * c - b + 2.0 * d
    poly_two = 2.0 * c + 5.0 * d - e
    curve_zero = a - 2.0 * b + c
    slope_zero = a - 4.0 * b + 3.0 * c
    curve_one = b - 2.0 * c + d
    slope_one = b - d
    curve_two = c - 2.0 * d + e
    slope_two = 3.0 * c - 4.0 * d + e
    big = 13.0 / 12.0
    smooth_zero = weno_eps + big * curve_zero * curve_zero + 0.25 * slope_zero * slope_zero
    smooth_one = weno_eps + big * curve_one * curve_one + 0.25 * slope_one * slope_one
    smooth_two = weno_eps + big * curve_two * curve_two + 0.25 * slope_two * slope_two
    zero_one = smooth_zero * smooth_one
    zero_two = smooth_zero * smooth_two
    one_two = smooth_one * smooth_two
    weight_zero = one_two * one_two
    weight_one = 6.0 * (zero_two * zero_two)
    weight_two = 3.0 * (zero_one * zero_one)
    return (weight_zero * poly_zero + weight_one * poly_one + weight_two * poly_two) / (
        6.0 * (weight_zero + weight_one + weight_two)
    )


def upwind_flux(at, speed):
    positive = speed >= 0.0
    minus_two, minus_one, center, one, two, three = [at(o) for o in range(-2, 4)]
    pick = functools.partial(jnp.where, positive)
    return speed * weno_one(
        pick(minus_two, three),
        pick(minus_one, two),
        pick(center, one),
        pick(one, center),
        pick(two, minus_one),
    )


def ring_sweep(values, advecting, axis):
    speed = 0.5 * (advecting + shift(advecting, 1, axis))
    flux = upwind_flux(lambda o: shift(values, o, axis), speed)
    return values * (speed - shift(speed, -1, axis)) - (flux - shift(flux, -1, axis))


def split_values(values):
    high = values.astype(jnp.bfloat16)
    return high, (values - high.astype(jnp.float32)).astype(jnp.bfloat16)


def narrow_dot(left, right, dims=((1,), (0,))):
    return lax.dot_general(
        left, right, (dims, ((), ())), preferred_element_type=jnp.float32
    )


def split_dot(left, right, dims=((1,), (0,))):
    joined_left = jnp.concatenate([left[0], left[0], left[1]], axis=dims[0][0])
    joined_right = jnp.concatenate([right[0], right[1], right[0]], axis=dims[1][0])
    return narrow_dot(joined_left, joined_right, dims)


def step_kernel(
    count_x,
    count_y,
    vel_far,
    green_far,
    labels_far,
    table_z_far,
    send_table_far,
    solve_in_far,
    solve_out_far,
    square_xy_far,
    square_z_far,
    take_table_far,
    turn_table_far,
    out_vel,
    out_green,
    out_frac,
    final,
    table_z,
    take_table,
    vel,
    green,
    labels,
    send_table,
    solve_in,
    solve_out,
    square_xy,
    square_z,
    turn_table,
    field,
    moved,
    pack,
    vel_pack,
    low_green,
    high_green,
    low_label,
    high_label,
    low_vel,
    high_vel,
    side,
    vel_near,
    vel_side,
    stress,
    stress_pack,
    stress_low,
    stress_high,
    stress_side,
    outbox,
    inbox,
    lines,
    backbox,
    homebox,
    load_sem,
    halo_sem,
    stress_sem,
    go_sem,
    back_sem,
):
    cells_x, cells_y, length_z = labels.shape
    devices = count_x * count_y
    rows = length_z // devices
    length_y = count_y * cells_y
    wide = cells_x + 4
    me_x = lax.axis_index("gx")
    me_y = lax.axis_index("gy")
    me = me_x * count_y + me_y
    mesh_type = pl.DeviceIdType.MESH

    turns = []
    for bit in range(count_x.bit_length() - 1):
        weight = 1 << bit
        turns.append(weight * (1 - 2 * lax.rem(me_x // weight, 2)))
    others = []
    for step in range(devices - 1, 0, -1):
        peer_x, peer_y = me_x, me_y
        for bit, turn in enumerate(turns):
            if (step // count_y) >> bit & 1:
                peer_x = peer_x + turn
        if step % count_y:
            peer_y = 1 - me_y
        others.append((peer_x * count_y + peer_y, (peer_x, peer_y)))

    barrier = pltpu.get_barrier_semaphore()
    for _, device in others:
        pl.semaphore_signal(barrier, inc=1, device_id=device, device_id_type=mesh_type)

    load_list = (
        (vel_far, vel),
        (green_far, green),
        (labels_far, labels),
        (table_z_far, table_z),
        (send_table_far.at[me_y], send_table),
        (square_xy_far, square_xy),
        (square_z_far.at[me], square_z),
        (solve_in_far, solve_in),
        (solve_out_far, solve_out),
        (take_table_far, take_table),
        (turn_table_far, turn_table),
    )
    loads = [
        pltpu.make_async_copy(source, target, load_sem.at[n])
        for n, (source, target) in enumerate(load_list)
    ]
    for copy in loads:
        copy.start()
    for copy in loads[:3]:
        copy.wait()

    fraction = labels[...].astype(jnp.float32) * 0.25
    for c in range(6):
        field[c] = green[c]
    field[6] = fraction
    row = lax.broadcasted_iota(jnp.int32, (cells_x, 8, length_z), 1)

    def fold(values):
        return jnp.where(row < 4, values[:, :8], values[:, cells_y - 8 :])

    for c in range(7):
        pack[c] = fold(field[c])
    for c in range(3):
        for x in range(cells_x):
            vel_pack[c, 2 * x] = vel[c, x, 0]
            vel_pack[c, 2 * x + 1] = vel[c, x, cells_y - 1]
            vel_side[c, x] = jnp.zeros((8, length_z), jnp.float32)

    pl.semaphore_wait(barrier, devices - 1)

    right = (lax.rem(me_x + 1, count_x), me_y)
    left = (lax.rem(me_x + count_x - 1, count_x), me_y)
    over = (me_x, lax.rem(me_y + 1, count_y))

    def remote(source, target, send_sem, recv_sem, device):
        return pltpu.make_async_remote_copy(
            src_ref=source,
            dst_ref=target,
            send_sem=send_sem,
            recv_sem=recv_sem,
            device_id=device,
            device_id_type=mesh_type,
        )

    halo_list = (
        (vel_pack, vel_near, over),
        (pack, side, over),
        (green.at[:, cells_x - 3 :], low_green, right),
        (green.at[:, :3], high_green, left),
        (vel.at[:, cells_x - 1 :], low_vel, right),
        (vel.at[:, :1], high_vel, left),
        (labels.at[cells_x - 3 :], low_label, right),
        (labels.at[:3], high_label, left),
    )
    halos = [
        remote(source, target, halo_sem.at[0, n], halo_sem.at[1, n], device)
        for n, (source, target, device) in enumerate(halo_list)
    ]
    for copy in halos:
        copy.start()

    def sweep_z(c, carry):
        for x in range(cells_x):
            moved[c, x] = ring_sweep(field[c, x], vel[2, x], 1)
        return carry

    lax.fori_loop(0, 7, sweep_z, 0)

    halos[0].wait()
    for c in range(3):
        for x in range(cells_x):
            vel_side[c, x, 0] = vel_near[c, 2 * x]
            vel_side[c, x, 7] = vel_near[c, 2 * x + 1]
    halos[1].wait()

    def sweep_y(c, carry):
        for x in range(cells_x):
            values = jnp.concatenate([field[c, x], side[c, x]], axis=0)
            advecting = jnp.concatenate([vel[1, x], vel_side[1, x]], axis=0)
            moved[c, x] = moved[c, x] + ring_sweep(values, advecting, 0)[:cells_y]
        return carry

    lax.fori_loop(0, 7, sweep_y, 0)

    for copy in halos[2:]:
        copy.wait()

    def wide_vel(c):
        return jnp.concatenate([low_vel[c], vel[c], high_vel[c]], axis=0)

    def sweep_x(values, c):
        advecting = [low_vel[0, 0]] + [vel[0, x] for x in range(cells_x)] + [high_vel[0, 0]]
        flux = []
        speeds = []
        for face in range(cells_x + 1):
            speed = 0.5 * (advecting[face] + advecting[face + 1])
            speeds.append(speed)
            flux.append(upwind_flux(lambda o: values[face + 2 + o], speed))
        for x in range(cells_x):
            moved[c, x] = (
                moved[c, x]
                + values[x + 3] * (speeds[x + 1] - speeds[x])
                - (flux[x + 1] - flux[x])
            )

    def sweep_green(c, carry):
        values = [low_green[c, n] for n in range(3)]
        values += [field[c, x] for x in range(cells_x)]
        values += [high_green[c, n] for n in range(3)]
        sweep_x(values, c)
        return carry

    lax.fori_loop(0, 6, sweep_green, 0)
    values = [low_label[n].astype(jnp.float32) * 0.25 for n in range(3)]
    values += [field[6, x] for x in range(cells_x)]
    values += [high_label[n].astype(jnp.float32) * 0.25 for n in range(3)]
    sweep_x(values, 6)

    def central_z(block):
        return 0.5 * (shift(block, 1, 2) - shift(block, -1, 2))

    def central_y(block, edge):
        ring = jnp.concatenate([block, edge], axis=1)
        return (0.5 * (shift(ring, 1, 1) - shift(ring, -1, 1)))[:, :cells_y]

    def central_x(ring):
        return 0.5 * (ring[2:] - ring[:-2])

    gradient = [
        [central_x(wide_vel(c)), central_y(vel[c], vel_side[c]), central_z(vel[c])]
        for c in range(3)
    ]
    old = [field[c] for c in range(6)]
    new = []
    for c in range(6):
        left_index, right_index = pair_list[c]
        stretch = None
        for inner in range(3):
            term = (
                gradient[left_index][inner] * old[slot_table[inner][right_index]]
                + old[slot_table[left_index][inner]] * gradient[right_index][inner]
            )
            stretch = term if stretch is None else stretch + term
        new.append(old[c] + time_step * (moved[c] + stretch))
        out_green[c] = new[c]
    new_fraction = field[6] + time_step * moved[6]
    out_frac[...] = new_fraction
    determinant = (
        new[0] * (new[1] * new[2] - new[5] * new[5])
        - new[3] * (new[3] * new[2] - new[5] * new[4])
        + new[4] * (new[3] * new[5] - new[1] * new[4])
    )
    dilate = dilation * (determinant - 1.0)
    scale = shear_modulus * new_fraction
    sigma = [scale * (new[c] - 1.0 + dilate) for c in range(3)]
    sigma += [scale * new[c] for c in range(3, 6)]
    xx, yy, zz, xy, xz, yz = sigma
    for n, part in enumerate((xx, xz, xy, yy, yz, zz)):
        stress[n] = part
    for n, part in enumerate((xy, yy, yz)):
        stress_pack[n] = fold(part)

    parts = (
        time_step * xx,
        2.0 * time_step * xy,
        vel[0] + 2.0 * time_step * central_z(xz),
        time_step * yy,
        vel[1] + 2.0 * time_step * central_z(yz),
        central_z(vel[2] + time_step * central_z(zz)),
    )
    stacked = jnp.concatenate(
        [part.reshape(cells_x * cells_y, length_z) for part in parts], axis=0
    )
    for copy in loads[3:]:
        copy.wait()
    modes_z = split_dot(table_z, split_values(stacked), ((1,), (1,)))
    modes_zy = split_dot(split_values(modes_z), send_table)
    for n in range(devices):
        outbox[n] = modes_zy[n * rows : (n + 1) * rows]

    for target, device in others:
        remote(outbox.at[target], inbox.at[me], go_sem.at[0], go_sem.at[1], device).start()
    inbox[me] = outbox[me]
    stress_list = (
        (stress_pack, stress_side, over),
        (stress.at[:3, cells_x - 1 :], stress_low, right),
        (stress.at[:3, :1], stress_high, left),
    )
    edges = [
        remote(source, target, stress_sem.at[0, n], stress_sem.at[1, n], device)
        for n, (source, target, device) in enumerate(stress_list)
    ]
    for copy in edges:
        copy.start()

    norm = square_xy[...] + square_z[...][None]
    live = norm > 0.0
    total = float(count_x * cells_x * length_y * length_z)
    green_function = jnp.where(live, (-1.0 / total) / jnp.where(live, norm, 1.0), 0.0)
    green_function = green_function.reshape(-1, length_y)

    most = pl.ds(0, devices - 1)
    remote(outbox.at[most], inbox.at[most], go_sem.at[0], go_sem.at[1], right).wait()

    for n in range(count_x):
        held = inbox[n * count_y]
        for m in range(1, count_y):
            held = held + inbox[n * count_y + m]
        lines[n * rows : (n + 1) * rows] = held
    arranged = jnp.concatenate(
        [lines[:, n * length_y : (n + 1) * length_y] for n in range(wide)], axis=0
    )
    pressure_modes = split_values(split_dot(solve_in, split_values(arranged)) * green_function)
    turned = (
        narrow_dot(pressure_modes[0], turn_table[0])
        + narrow_dot(pressure_modes[0], turn_table[1])
        + narrow_dot(pressure_modes[1], turn_table[0])
    )
    pressure = split_dot(solve_out, split_values(turned))
    height = count_x * rows
    near_y = cells_y + 2
    for m in range(count_y):
        spread = jnp.concatenate(
            [
                pressure[n * height : (n + 1) * height, m * near_y : (m + 1) * near_y]
                for n in range(cells_x + 2)
            ]
            + [jnp.zeros((height, backbox.shape[2] - (cells_x + 2) * near_y), jnp.float32)],
            axis=1,
        )
        for n in range(count_x):
            backbox[n * count_y + m] = spread[n * rows : (n + 1) * rows]

    for target, device in others:
        remote(
            backbox.at[target], homebox.at[me], back_sem.at[0], back_sem.at[1], device
        ).start()
    homebox[me] = backbox[me]

    for copy in edges:
        copy.wait()
    force = (
        (0, 2, 0, 1),
        (2, 3, 1, 4),
        (1, 4, 2, 5),
    )
    for c, (part_x, part_y, edge_y, part_z) in enumerate(force):
        ring = jnp.concatenate([stress_low[part_x], stress[part_x], stress_high[part_x]], axis=0)
        pushed = (
            central_x(ring)
            + central_y(stress[part_y], stress_side[edge_y])
            + central_z(stress[part_z])
        )
        out_vel[c] = vel[c] + time_step * pushed

    remote(backbox.at[most], homebox.at[most], back_sem.at[0], back_sem.at[1], right).wait()
    for n in range(devices):
        final[n * rows : (n + 1) * rows] = homebox[n]


def finish_kernel(
    predicted,
    green,
    fraction,
    final,
    table_z,
    take_table,
    out_vel,
    out_green,
    out_frac,
    vel,
    sems,
):
    store_green = pltpu.make_async_copy(green, out_green, sems.at[0])
    store_frac = pltpu.make_async_copy(fraction, out_frac, sems.at[1])
    store_green.start()
    store_frac.start()
    taken = jnp.concatenate([take_table[...], take_table[...]], axis=1)
    slopes = narrow_dot(taken, jnp.concatenate(split_values(final[...]), axis=1), ((1,), (1,)))
    slopes = split_dot(split_values(slopes), table_z).reshape(predicted.shape)
    vel[0] = predicted[0] - slopes[0]
    vel[1] = predicted[1] - slopes[1]
    vel[2] = predicted[2] - 0.5 * (shift(slopes[2], 1, 2) - shift(slopes[2], -1, 2))
    store_vel = pltpu.make_async_copy(vel, out_vel, sems.at[2])
    store_vel.start()
    store_vel.wait()
    store_green.wait()
    store_frac.wait()


def fused_local(count_x, count_y, velocity, cauchy_green, labels):
    cells_x, cells_y, length_z = labels.shape
    devices = count_x * count_y
    rows = length_z // devices
    length_y = count_y * cells_y
    tables = spectral_tables(count_x, count_y, cells_x, cells_y, length_z)
    wide = (cells_x + 4) * length_y
    back = back_lanes(cells_x, cells_y)
    plane = (cells_y, length_z)
    real = functools.partial(pltpu.VMEM, dtype=jnp.float32)
    outputs = (
        jax.ShapeDtypeStruct(velocity.shape, jnp.float32),
        jax.ShapeDtypeStruct(cauchy_green.shape, jnp.float32),
        jax.ShapeDtypeStruct(labels.shape, jnp.float32),
    )
    handed = outputs + (
        jax.ShapeDtypeStruct((length_z, back), jnp.float32),
        jax.ShapeDtypeStruct(tables[0].shape, jnp.bfloat16),
        jax.ShapeDtypeStruct(tables[6].shape, jnp.bfloat16),
    )
    near = pl.BlockSpec(memory_space=pltpu.VMEM)
    far = pl.BlockSpec(memory_space=pltpu.HBM)
    scratch = [
        real(velocity.shape),
        real(cauchy_green.shape),
        pltpu.VMEM(labels.shape, jnp.int32),
        pltpu.VMEM(tables[1].shape[1:], jnp.bfloat16),
        pltpu.VMEM(tables[2].shape, jnp.bfloat16),
        pltpu.VMEM(tables[3].shape, jnp.bfloat16),
        real(tables[4].shape),
        real(tables[5].shape[1:]),
        pltpu.VMEM(tables[7].shape, jnp.bfloat16),
        real((7, cells_x) + plane),
        real((7, cells_x) + plane),
        real((7, cells_x, 8, length_z)),
        real((3, 2 * cells_x, length_z)),
        real((6, 3) + plane),
        real((6, 3) + plane),
        pltpu.VMEM((3,) + plane, jnp.int32),
        pltpu.VMEM((3,) + plane, jnp.int32),
        real((3, 1) + plane),
        real((3, 1) + plane),
        real((7, cells_x, 8, length_z)),
        real((3, 2 * cells_x, length_z)),
        real((3, cells_x, 8, length_z)),
        real((6, cells_x) + plane),
        real((3, cells_x, 8, length_z)),
        real((3, 1) + plane),
        real((3, 1) + plane),
        real((3, cells_x, 8, length_z)),
        real((devices, rows, wide)),
        real((devices, rows, wide)),
        real((count_x * rows, wide)),
        real((devices, rows, back)),
        real((devices, rows, back)),
        pltpu.SemaphoreType.DMA((11,)),
        pltpu.SemaphoreType.DMA((2, 8)),
        pltpu.SemaphoreType.DMA((2, 3)),
        pltpu.SemaphoreType.DMA((2,)),
        pltpu.SemaphoreType.DMA((2,)),
    ]
    made = pl.pallas_call(
        functools.partial(step_kernel, count_x, count_y),
        out_shape=handed,
        in_specs=[far] * 11,
        out_specs=(near,) * 6,
        scratch_shapes=scratch,
        compiler_params=pltpu.CompilerParams(
            collective_id=0, has_side_effects=True, vmem_limit_bytes=32 * 1024 * 1024
        ),
        name="membrane_step",
    )(*[
        pltpu.with_memory_space_constraint(value, pltpu.HBM)
        for value in (velocity, cauchy_green, labels, *map(jnp.asarray, tables))
    ])
    return tuple(
        pl.pallas_call(
            finish_kernel,
            out_shape=outputs,
            in_specs=[near] * 6,
            out_specs=(far,) * 3,
            scratch_shapes=[real(velocity.shape), pltpu.SemaphoreType.DMA((3,))],
            compiler_params=pltpu.CompilerParams(vmem_limit_bytes=16 * 1024 * 1024),
            name="finish_step",
        )(*made)
    )


def fits_fused(count_x, count_y, shape):
    _, length_x, length_y, length_z = shape
    cells_x, cells_y = length_x // count_x, length_y // count_y
    devices = count_x * count_y
    return (
        count_y == 2
        and count_x > 2
        and count_x & (count_x - 1) == 0
        and length_z % 128 == 0
        and length_z % devices == 0
        and length_z // devices in (4, 8)
        and cells_x >= 4
        and cells_y % 8 == 0
        and cells_y >= 8
        and (cells_x + 4) * length_y % 128 == 0
        and length_x * length_y <= 4096
    )


def solution(mesh):
    placed = (P(None, "gx", "gy", None), P(None, "gx", "gy", None), P("gx", "gy", None))
    count_x, count_y = mesh.shape["gx"], mesh.shape["gy"]

    def step(velocity, cauchy_green, labels):
        if fits_fused(count_x, count_y, velocity.shape):
            body = functools.partial(fused_local, count_x, count_y)
        else:
            body = local
        return jax.shard_map(
            body, mesh=mesh, in_specs=placed, out_specs=placed, check_vma=False
        )(velocity, cauchy_green, labels)

    return step
```

```python
import functools
import math

import jax
import jax.numpy as jnp
import numpy as np
from jax import lax
from jax.experimental import pallas as pl
from jax.experimental.pallas import tpu as pltpu
from jax.sharding import PartitionSpec as P

time_step = 0.1
shear_modulus = 4.0
dilation = 0.5
weno_eps = 1e-06
pair_list = ((0, 0), (1, 1), (2, 2), (0, 1), (0, 2), (1, 2))
slot_table = ((0, 3, 4), (3, 1, 5), (4, 5, 2))
plane_bits = 2


def padded_2(block, sides, width):
    for axis, dim in sides:
        count = lax.axis_size(axis)
        forward = [(i, i + 1) for i in range(count - 1)]
        forward.append((count - 1, 0))
        backward = [(target, source) for source, target in forward]
        low = lax.ppermute(
            lax.slice_in_dim(block, block.shape[dim] - width, None, axis=dim), axis, forward
        )
        high = lax.ppermute(lax.slice_in_dim(block, 0, width, axis=dim), axis, backward)
        block = jnp.concatenate([low, block, high], axis=dim)
    return block


def weno_face(minus_two, minus_one, center, plus_one, plus_two):
    poly_zero = (2.0 * minus_two - 7.0 * minus_one + 11.0 * center) / 6.0
    poly_one = (-minus_one + 5.0 * center + 2.0 * plus_one) / 6.0
    poly_two = (2.0 * center + 5.0 * plus_one - plus_two) / 6.0
    curve_zero = minus_two - 2.0 * minus_one + center
    slope_zero = minus_two - 4.0 * minus_one + 3.0 * center
    curve_one = minus_one - 2.0 * center + plus_one
    slope_one = minus_one - plus_one
    curve_two = center - 2.0 * plus_one + plus_two
    slope_two = 3.0 * center - 4.0 * plus_one + plus_two
    smooth_zero = weno_eps + 13.0 / 12.0 * curve_zero * curve_zero + 0.25 * slope_zero * slope_zero
    smooth_one = weno_eps + 13.0 / 12.0 * curve_one * curve_one + 0.25 * slope_one * slope_one
    smooth_two = weno_eps + 13.0 / 12.0 * curve_two * curve_two + 0.25 * slope_two * slope_two
    weight_zero = 0.1 / (smooth_zero * smooth_zero)
    weight_one = 0.6 / (smooth_one * smooth_one)
    weight_two = 0.3 / (smooth_two * smooth_two)
    return (weight_zero * poly_zero + weight_one * poly_one + weight_two * poly_two) / (
        weight_zero + weight_one + weight_two
    )


def face_flux(shifted, speed_face):
    upwind_left = weno_face(shifted(-2), shifted(-1), shifted(0), shifted(1), shifted(2))
    upwind_right = weno_face(shifted(3), shifted(2), shifted(1), shifted(0), shifted(-1))
    return speed_face * jnp.where(speed_face >= 0.0, upwind_left, upwind_right)


def sweep(quantity, advecting, sweep_dim, anchor, count):

    def shifted(offset):
        return lax.slice_in_dim(
            quantity, anchor - 1 + offset, anchor + offset + count, axis=sweep_dim
        )

    speed_face = 0.5 * (
        lax.slice_in_dim(advecting, anchor - 1, anchor + count, axis=sweep_dim - 1)
        + lax.slice_in_dim(advecting, anchor, anchor + count + 1, axis=sweep_dim - 1)
    )
    flux_face = face_flux(shifted, speed_face)
    flux_upper = lax.slice_in_dim(flux_face, 1, count + 1, axis=sweep_dim)
    flux_lower = lax.slice_in_dim(flux_face, 0, count, axis=sweep_dim)
    center = lax.slice_in_dim(quantity, anchor, anchor + count, axis=sweep_dim)
    spread = lax.slice_in_dim(speed_face, 1, count + 1, axis=sweep_dim - 1) - lax.slice_in_dim(
        speed_face, 0, count, axis=sweep_dim - 1
    )
    return center * spread - (flux_upper - flux_lower)


def sweep_periodic(quantity, advecting):

    def shifted(offset):
        return jnp.roll(quantity, -offset, 3)

    speed_face = 0.5 * (advecting + jnp.roll(advecting, -1, 2))
    flux_face = face_flux(shifted, speed_face)
    return quantity * (speed_face - jnp.roll(speed_face, 1, 2)) - (
        flux_face - jnp.roll(flux_face, 1, 3)
    )


def region_gradient(padded, anchor, count_x, count_y):
    gradient = []
    for component in range(3):
        advecting = padded[7 + component]
        center = advecting[anchor : anchor + count_x, anchor : anchor + count_y]
        along_x = 0.5 * (
            advecting[anchor + 1 : anchor + 1 + count_x, anchor : anchor + count_y]
            - advecting[anchor - 1 : anchor - 1 + count_x, anchor : anchor + count_y]
        )
        along_y = 0.5 * (
            advecting[anchor : anchor + count_x, anchor + 1 : anchor + 1 + count_y]
            - advecting[anchor : anchor + count_x, anchor - 1 : anchor - 1 + count_y]
        )
        along_z = 0.5 * (jnp.roll(center, -1, 2) - jnp.roll(center, 1, 2))
        gradient.append([along_x, along_y, along_z])
    return gradient


def advance(green, fraction, transported, gradient):
    updated = []
    for component in range(6):
        left_index, right_index = pair_list[component]
        stretch = jnp.zeros_like(green[0])
        for inner_index in range(3):
            stretch = (
                stretch
                + gradient[left_index][inner_index] * green[slot_table[inner_index][right_index]]
            )
            stretch = (
                stretch
                + green[slot_table[left_index][inner_index]] * gradient[right_index][inner_index]
            )
        updated.append(green[component] + time_step * (transported[component] + stretch))
    return (jnp.stack(updated), fraction + time_step * transported[6])


def membrane_stress(green, fraction):
    determinant = (
        green[0] * (green[1] * green[2] - green[5] * green[5])
        - green[3] * (green[3] * green[2] - green[5] * green[4])
        + green[4] * (green[3] * green[5] - green[1] * green[4])
    )
    dilate = dilation * (determinant - 1.0)
    stress_parts = []
    for component in range(6):
        if component < 3:
            stress_parts.append(green[component] - 1.0 + dilate)
        else:
            stress_parts.append(green[component])
    return shear_modulus * fraction * jnp.stack(stress_parts)


def update_region(padded, anchor, count_x, count_y):
    carried = padded[:7]
    transported = sweep(
        carried[:, :, anchor : anchor + count_y],
        padded[7, :, anchor : anchor + count_y],
        1,
        anchor,
        count_x,
    )
    transported = transported + sweep(
        carried[:, anchor : anchor + count_x],
        padded[8, anchor : anchor + count_x],
        2,
        anchor,
        count_y,
    )
    region = padded[:, anchor : anchor + count_x, anchor : anchor + count_y]
    transported = transported + sweep_periodic(region[:7], region[9])
    gradient = region_gradient(padded, anchor, count_x, count_y)
    new_green, new_fraction = advance(region[:6], region[6], transported, gradient)
    return (new_green, new_fraction, membrane_stress(new_green, new_fraction))


def derive_x(widened):
    return 0.5 * (widened[..., 2:, 1:-1, :] - widened[..., :-2, 1:-1, :])


def derive_y(widened):
    return 0.5 * (widened[..., 1:-1, 2:, :] - widened[..., 1:-1, :-2, :])


def derive_z(widened):
    inside = widened[..., 1:-1, 1:-1, :]
    return 0.5 * (jnp.roll(inside, -1, -1) - jnp.roll(inside, 1, -1))


def stress_force(widened):
    return jnp.stack(
        [
            derive_x(widened[slot_table[index_row][0]])
            + derive_y(widened[slot_table[index_row][1]])
            + derive_z(widened[slot_table[index_row][2]])
            for index_row in range(3)
        ]
    )


def dft_tables(length):
    wave_index = jnp.arange(length, dtype=jnp.int32)
    phase_index = wave_index[:, None] * wave_index[None, :] % length
    angle_table = 2.0 * math.pi / length * phase_index.astype(jnp.float32)
    return (jnp.cos(angle_table), jnp.sin(angle_table))


def contract(einsum_form, values, dft_table):
    return jnp.einsum(einsum_form, values, dft_table, precision=lax.Precision.HIGHEST)


def forward_transform(cell_field):
    components, cells_x, cells_y, length_z = cell_field.shape
    length_x = cells_x * lax.axis_size("gx")
    length_y = cells_y * lax.axis_size("gy")
    slab_z = length_z // lax.axis_size("gx")
    cosine_z, sine_z = dft_tables(length_z)
    real_z = contract("cxyz,zk->cxyk", cell_field, cosine_z)
    imag_z = -contract("cxyz,zk->cxyk", cell_field, sine_z)
    lines_x = lax.all_to_all(
        jnp.stack([real_z, imag_z], 1), "gx", split_axis=4, concat_axis=2, tiled=True
    )
    lines_x = lines_x.reshape(components, 2, length_x, cells_y * slab_z)
    cosine_x, sine_x = dft_tables(length_x)
    real_part = lines_x[:, 0]
    imag_part = lines_x[:, 1]
    real_x = contract("cxm,xk->ckm", real_part, cosine_x) + contract(
        "cxm,xk->ckm", imag_part, sine_x
    )
    imag_x = contract("cxm,xk->ckm", imag_part, cosine_x) - contract(
        "cxm,xk->ckm", real_part, sine_x
    )
    paired_x = jnp.stack([real_x, imag_x], 1).reshape(components, 2, length_x, cells_y, slab_z)
    lines_y = lax.all_to_all(paired_x, "gy", split_axis=2, concat_axis=3, tiled=True)
    cosine_y, sine_y = dft_tables(length_y)
    real_part = lines_y[:, 0]
    imag_part = lines_y[:, 1]
    real_y = contract("cayz,yk->ckaz", real_part, cosine_y) + contract(
        "cayz,yk->ckaz", imag_part, sine_y
    )
    imag_y = contract("cayz,yk->ckaz", imag_part, cosine_y) - contract(
        "cayz,yk->ckaz", real_part, sine_y
    )
    return (real_y, imag_y)


def inverse_transform(real_k, imag_k, cells_y, length_z):
    components, length_y, block_x, slab_z = real_k.shape
    length_x = block_x * lax.axis_size("gy")
    cosine_y, sine_y = dft_tables(length_y)
    real_y = contract("ckaz,ky->cayz", real_k, cosine_y) - contract("ckaz,ky->cayz", imag_k, sine_y)
    imag_y = contract("ckaz,ky->cayz", real_k, sine_y) + contract("ckaz,ky->cayz", imag_k, cosine_y)
    lines_x = lax.all_to_all(
        jnp.stack([real_y, imag_y], 1), "gy", split_axis=3, concat_axis=2, tiled=True
    )
    lines_x = lines_x.reshape(components, 2, length_x, cells_y * slab_z)
    cosine_x, sine_x = dft_tables(length_x)
    real_part = lines_x[:, 0]
    imag_part = lines_x[:, 1]
    real_x = contract("ckm,kx->cxm", real_part, cosine_x) - contract(
        "ckm,kx->cxm", imag_part, sine_x
    )
    imag_x = contract("ckm,kx->cxm", real_part, sine_x) + contract(
        "ckm,kx->cxm", imag_part, cosine_x
    )
    paired_x = jnp.stack([real_x, imag_x], 1).reshape(components, 2, length_x, cells_y, slab_z)
    slab_pairs = lax.all_to_all(paired_x, "gx", split_axis=2, concat_axis=4, tiled=True)
    cosine_z, sine_z = dft_tables(length_z)
    result = contract("cxyk,kz->cxyz", slab_pairs[:, 0], cosine_z) - contract(
        "cxyk,kz->cxyz", slab_pairs[:, 1], sine_z
    )
    return result / float(length_x * length_y * length_z)


def sine_numbers(wave_index, length):
    silent = wave_index % (length // 2) == 0
    sine_value = jnp.sin(2.0 * math.pi / length * wave_index.astype(jnp.float32))
    return (jnp.where(silent, 0.0, sine_value), silent)


def wave_numbers(length_y, block_x, slab_z, length_x, length_z):
    index_y = jnp.arange(length_y, dtype=jnp.int32)
    index_x = lax.axis_index("gy") * block_x + jnp.arange(block_x, dtype=jnp.int32)
    index_z = lax.axis_index("gx") * slab_z + jnp.arange(slab_z, dtype=jnp.int32)
    sine_x, silent_x = sine_numbers(index_x, length_x)
    sine_y, silent_y = sine_numbers(index_y, length_y)
    sine_z, silent_z = sine_numbers(index_z, length_z)
    live_mode = jnp.logical_not(
        silent_y[:, None, None] & silent_x[None, :, None] & silent_z[None, None, :]
    )
    return ((sine_x[None, :, None], sine_y[:, None, None], sine_z[None, None, :]), live_mode)


def local(velocity, cauchy_green, labels):
    cells_x = velocity.shape[1]
    cells_y = velocity.shape[2]
    length_z = velocity.shape[3]
    fraction = labels.astype(jnp.float32) * 0.25
    stacked = jnp.concatenate([cauchy_green, fraction[None], velocity], 0)
    padded = padded_2(stacked, (("gx", 1), ("gy", 2)), 4)
    green_wide, fraction_wide, stress_wide = update_region(padded, 3, cells_x + 2, cells_y + 2)
    new_green = green_wide[:, 1:-1, 1:-1]
    new_fraction = fraction_wide[1:-1, 1:-1]
    predicted = velocity + time_step * stress_force(stress_wide)
    length_x = cells_x * lax.axis_size("gx")
    velocity_wide = padded_2(predicted, (("gx", 1), ("gy", 2)), 1)
    divergence = (
        derive_x(velocity_wide[0]) + derive_y(velocity_wide[1]) + derive_z(velocity_wide[2])
    )
    real_k, imag_k = forward_transform(divergence[None])
    sine_list, live_mode = wave_numbers(
        real_k.shape[1], real_k.shape[2], real_k.shape[3], length_x, length_z
    )
    norm_sq = (
        sine_list[0] * sine_list[0] + sine_list[1] * sine_list[1] + sine_list[2] * sine_list[2]
    )
    safe_norm = jnp.where(live_mode, norm_sq, 1.0)
    pressure_real = jnp.where(live_mode, -real_k[0] / safe_norm, 0.0)
    pressure_imag = jnp.where(live_mode, -imag_k[0] / safe_norm, 0.0)
    pressure = inverse_transform(pressure_real[None], pressure_imag[None], cells_y, length_z)
    pressure_wide = padded_2(pressure, (("gx", 1), ("gy", 2)), 1)
    new_velocity = predicted - jnp.stack(
        [derive_x(pressure_wide[0]), derive_y(pressure_wide[0]), derive_z(pressure_wide[0])]
    )
    return (new_velocity, new_green, new_fraction)


def hartley(length):
    index = np.arange(length)
    angle = 2.0 * np.pi / length * (np.outer(index, index) % length)
    return np.cos(angle) + np.sin(angle)


def sine_squares(length):
    index = np.arange(length)
    sine = np.where(index % (length // 2) == 0, 0.0, np.sin(2.0 * np.pi / length * index))
    return sine * sine


def split_table(table):
    high = np.asarray(table, jnp.bfloat16)
    low = np.asarray(table - np.asarray(high, np.float64), jnp.bfloat16)
    return np.stack([high, low])


def back_lanes(cells_x, cells_y):
    return -(-(cells_x + 2) * (cells_y + 2) // 128) * 128


def spectral_tables(count_x, count_y, cells_x, cells_y, length_z):
    length_x, length_y = count_x * cells_x, count_y * cells_y
    devices = count_x * count_y
    rows = length_z // devices
    table_x, table_y, table_z = hartley(length_x), hartley(length_y), hartley(length_z)
    wide = cells_x + 4
    stencils = (
        {0: 1.0},
        {-1: 0.5, 1: -0.5},
        {-2: 0.25, 0: -0.5, 2: 0.25},
    )
    field_orders = ((2, 0), (1, 1), (1, 0), (0, 2), (0, 1), (0, 0))
    send_table = np.zeros((count_y, 6, cells_x, cells_y, wide, length_y))
    near_x, near_y = cells_x + 2, cells_y + 2
    take_table = np.zeros((3, cells_x, cells_y, back_lanes(cells_x, cells_y)))
    turn_table = np.zeros((length_y, count_y, near_y))
    for block in range(count_y):
        place = block * cells_y + np.arange(cells_y)
        along = [
            sum(w * table_y[(place + o) % length_y] for o, w in stencil.items())
            for stencil in stencils
        ]
        for field, (order_x, order_y) in enumerate(field_orders):
            for cell in range(cells_x):
                for offset, weight in stencils[order_x].items():
                    send_table[block, field, cell, :, cell + 2 + offset] += weight * along[order_y]
        ring = (block * cells_y + np.arange(near_y) - 1) % length_y
        turn_table[:, block] = table_y[:, ring]
    for x in range(cells_x):
        for y in range(cells_y):
            place = (x + 1) * near_y + y + 1
            take_table[0, x, y, place + near_y] = 0.5
            take_table[0, x, y, place - near_y] = -0.5
            take_table[1, x, y, place + 1] = 0.5
            take_table[1, x, y, place - 1] = -0.5
            take_table[2, x, y, place] = 1.0
    same = np.eye(rows)
    reach = (
        np.arange(count_x)[None, :] * cells_x + np.arange(wide)[:, None] - 2
    ) % length_x
    solve_in = np.einsum("kib,qr->kqibr", table_x[:, reach], same).reshape(
        length_x * rows, wide * count_x * rows
    )
    home = np.arange(count_x)[None, :] * cells_x + np.arange(near_x)[:, None] - 1
    solve_out = np.einsum("ibk,qr->ibqkr", table_x[home % length_x], same).reshape(
        near_x * count_x * rows, length_x * rows
    )
    square_xy = np.repeat(sine_squares(length_x), rows)[:, None] + sine_squares(length_y)[None, :]
    square_z = sine_squares(length_z).reshape(devices, rows)
    square_z = np.tile(square_z, (1, 8 // rows))[:, :, None] * np.ones((1, 1, length_y))
    send_table = send_table.reshape(count_y, 6 * cells_x * cells_y, wide * length_y)
    take_table = take_table.reshape(3 * cells_x * cells_y, -1)
    return (
        split_table(table_z),
        np.moveaxis(split_table(send_table), 0, 1),
        split_table(solve_in),
        split_table(solve_out),
        np.asarray(square_xy.reshape(-1, 8, length_y), np.float32),
        np.asarray(square_z, np.float32),
        np.asarray(take_table, jnp.bfloat16),
        split_table(turn_table.reshape(length_y, count_y * near_y)),
    )


def shift(values, offset, axis):
    extent = values.shape[axis]
    if offset % extent == 0:
        return values
    return pltpu.roll(values, (-offset) % extent, axis)


def weno_one(a, b, c, d, e):
    poly_zero = 2.0 * a - 7.0 * b + 11.0 * c
    poly_one = 5.0 * c - b + 2.0 * d
    poly_two = 2.0 * c + 5.0 * d - e
    curve_zero = a - 2.0 * b + c
    slope_zero = a - 4.0 * b + 3.0 * c
    curve_one = b - 2.0 * c + d
    slope_one = b - d
    curve_two = c - 2.0 * d + e
    slope_two = 3.0 * c - 4.0 * d + e
    big = 13.0 / 12.0
    smooth_zero = weno_eps + big * curve_zero * curve_zero + 0.25 * slope_zero * slope_zero
    smooth_one = weno_eps + big * curve_one * curve_one + 0.25 * slope_one * slope_one
    smooth_two = weno_eps + big * curve_two * curve_two + 0.25 * slope_two * slope_two
    zero_one = smooth_zero * smooth_one
    zero_two = smooth_zero * smooth_two
    one_two = smooth_one * smooth_two
    weight_zero = one_two * one_two
    weight_one = 6.0 * (zero_two * zero_two)
    weight_two = 3.0 * (zero_one * zero_one)
    return (weight_zero * poly_zero + weight_one * poly_one + weight_two * poly_two) / (
        6.0 * (weight_zero + weight_one + weight_two)
    )


def upwind_flux(at, speed):
    positive = speed >= 0.0
    minus_two, minus_one, center, one, two, three = [at(o) for o in range(-2, 4)]
    pick = functools.partial(jnp.where, positive)
    return speed * weno_one(
        pick(minus_two, three),
        pick(minus_one, two),
        pick(center, one),
        pick(one, center),
        pick(two, minus_one),
    )


def ring_sweep(values, advecting, axis):
    speed = 0.5 * (advecting + shift(advecting, 1, axis))
    flux = upwind_flux(lambda o: shift(values, o, axis), speed)
    return values * (speed - shift(speed, -1, axis)) - (flux - shift(flux, -1, axis))


def split_values(values):
    high = values.astype(jnp.bfloat16)
    return high, (values - high.astype(jnp.float32)).astype(jnp.bfloat16)


def narrow_dot(left, right, dims=((1,), (0,))):
    return lax.dot_general(
        left, right, (dims, ((), ())), preferred_element_type=jnp.float32
    )


def split_dot(left, right, dims=((1,), (0,))):
    joined_left = jnp.concatenate([left[0], left[0], left[1]], axis=dims[0][0])
    joined_right = jnp.concatenate([right[0], right[1], right[0]], axis=dims[1][0])
    return narrow_dot(joined_left, joined_right, dims)


def step_kernel(
    count_x,
    count_y,
    vel_far,
    green_far,
    labels_far,
    table_z_far,
    send_table_far,
    solve_in_far,
    solve_out_far,
    square_xy_far,
    square_z_far,
    take_table_far,
    turn_table_far,
    out_vel,
    out_green,
    out_frac,
    final,
    table_z,
    take_table,
    vel,
    green,
    labels,
    send_table,
    solve_in,
    solve_out,
    square_xy,
    square_z,
    turn_table,
    field,
    moved,
    pack,
    vel_pack,
    low_green,
    high_green,
    low_label,
    high_label,
    low_vel,
    high_vel,
    side,
    vel_near,
    vel_side,
    stress,
    stress_pack,
    stress_low,
    stress_high,
    stress_side,
    outbox,
    inbox,
    lines,
    backbox,
    homebox,
    load_sem,
    halo_sem,
    stress_sem,
    go_sem,
    back_sem,
    rung_sem,
    edge_flux,
):
    cells_x, cells_y, length_z = labels.shape
    devices = count_x * count_y
    rows = length_z // devices
    length_y = count_y * cells_y
    wide = cells_x + 4
    me_x = lax.axis_index("gx")
    me_y = lax.axis_index("gy")
    me = me_x * count_y + me_y
    mesh_type = pl.DeviceIdType.MESH

    turns = []
    for bit in range(count_x.bit_length() - 1):
        weight = 1 << bit
        turns.append(weight * (1 - 2 * lax.rem(me_x // weight, 2)))
    others = []
    for step in range(devices - 1, 0, -1):
        peer_x, peer_y = me_x, me_y
        for bit, turn in enumerate(turns):
            if (step // count_y) >> bit & 1:
                peer_x = peer_x + turn
        if step % count_y:
            peer_y = 1 - me_y
        others.append((peer_x * count_y + peer_y, (peer_x, peer_y)))

    def toggled(mask, flip):
        place = me_x
        for bit, turn in enumerate(turns):
            if mask >> bit & 1:
                place = place + turn
        return (place, 1 - me_y if flip else me_y)

    right = (lax.rem(me_x + 1, count_x), me_y)
    left = (lax.rem(me_x + count_x - 1, count_x), me_y)
    over = (me_x, 1 - me_y)
    rungs = [toggled(1 << bit, False) for bit in range(plane_bits, len(turns))]
    mates = [toggled(mask, flip) for mask in range(1 << plane_bits) for flip in (0, 1)][1:]
    greeted = [left, right] + rungs + mates
    barrier = pltpu.get_barrier_semaphore()
    for device in greeted:
        pl.semaphore_signal(barrier, inc=1, device_id=device, device_id_type=mesh_type)

    load_list = (
        (vel_far, vel),
        (green_far, green),
        (labels_far, labels),
        (table_z_far, table_z),
        (send_table_far.at[me_y], send_table),
        (square_xy_far, square_xy),
        (square_z_far.at[me], square_z),
        (solve_in_far, solve_in),
        (solve_out_far, solve_out),
        (take_table_far, take_table),
        (turn_table_far, turn_table),
    )
    loads = [
        pltpu.make_async_copy(source, target, load_sem.at[n])
        for n, (source, target) in enumerate(load_list)
    ]
    for copy in loads:
        copy.start()
    for copy in loads[:3]:
        copy.wait()

    fraction = labels[...].astype(jnp.float32) * 0.25
    for c in range(6):
        field[c] = green[c]
    field[6] = fraction
    row = lax.broadcasted_iota(jnp.int32, (cells_x, 8, length_z), 1)

    def fold(values):
        return jnp.where(row < 4, values[:, :8], values[:, cells_y - 8 :])

    for c in range(7):
        pack[c] = fold(field[c])
    for c in range(3):
        for x in range(cells_x):
            vel_pack[c, 2 * x] = vel[c, x, 0]
            vel_pack[c, 2 * x + 1] = vel[c, x, cells_y - 1]
            vel_side[c, x] = jnp.zeros((8, length_z), jnp.float32)

    def sweep_z(c, carry):
        for x in range(cells_x):
            moved[c, x] = ring_sweep(field[c, x], vel[2, x], 1)
        return carry

    @pl.when(me_x == 0)
    def _():
        lax.fori_loop(0, 7, sweep_z, 0)

    pl.semaphore_wait(barrier, len(greeted))


    def remote(source, target, send_sem, recv_sem, device):
        return pltpu.make_async_remote_copy(
            src_ref=source,
            dst_ref=target,
            send_sem=send_sem,
            recv_sem=recv_sem,
            device_id=device,
            device_id_type=mesh_type,
        )

    halo_list = (
        (vel_pack, vel_near, over),
        (pack, side, over),
        (vel.at[:, :1], high_vel, left),
        (labels.at[:3], high_label, left),
        *[
            (green.at[n : n + 2, :3], high_green.at[n : n + 2], left)
            for n in range(0, 6, 2)
        ],
        (vel.at[:, cells_x - 1 :], low_vel, right),
        (labels.at[cells_x - 3 :], low_label, right),
        (green.at[:, cells_x - 3 :], low_green, right),
    )
    halos = [
        remote(source, target, halo_sem.at[0, n], halo_sem.at[1, n], device)
        for n, (source, target, device) in enumerate(halo_list)
    ]
    for copy in halos:
        copy.start()

    def tell(n):
        pl.semaphore_signal(rung_sem.at[n], inc=1, device_id=rungs[n], device_id_type=mesh_type)

    if rungs:
        tell(0)

    @pl.when(me_x != 0)
    def _():
        lax.fori_loop(0, 7, sweep_z, 0)

    halos[0].wait()
    for c in range(3):
        for x in range(cells_x):
            vel_side[c, x, 0] = vel_near[c, 2 * x]
            vel_side[c, x, 7] = vel_near[c, 2 * x + 1]
    for n in range(1, len(rungs)):
        pl.semaphore_wait(rung_sem.at[n - 1], 1)
        tell(n)
    halos[1].wait()

    def sweep_y(c, carry):
        for x in range(cells_x):
            values = jnp.concatenate([field[c, x], side[c, x]], axis=0)
            advecting = jnp.concatenate([vel[1, x], vel_side[1, x]], axis=0)
            moved[c, x] = moved[c, x] + ring_sweep(values, advecting, 0)[:cells_y]
        return carry

    lax.fori_loop(0, 7, sweep_y, 0)

    for copy in halos[7:]:
        copy.wait()

    def wide_vel(c):
        return jnp.concatenate([low_vel[c], vel[c], high_vel[c]], axis=0)

    def plane_at(c, n):
        if n < 3:
            return low_label[n].astype(jnp.float32) * 0.25 if c is None else low_green[c, n]
        if n < cells_x + 3:
            return field[6 if c is None else c, n - 3]
        n = n - cells_x - 3
        return high_label[n].astype(jnp.float32) * 0.25 if c is None else high_green[c, n]

    def face_speed(face):
        before = low_vel[0, 0] if face == 0 else vel[0, face - 1]
        after = high_vel[0, 0] if face == cells_x else vel[0, face]
        return 0.5 * (before + after)

    split_face = cells_x - 2

    def face_flux_x(c, face, speed):
        return upwind_flux(lambda o: plane_at(c, face + 2 + o), speed)

    def sweep_faces(c, first, last, speed_low, flux_low):
        slot = 6 if c is None else c
        for face in range(first, last):
            speed = face_speed(face)
            flux = face_flux_x(c, face, speed)
            if flux_low is not None:
                moved[slot, face - 1] = (
                    moved[slot, face - 1]
                    + plane_at(c, face + 2) * (speed - speed_low)
                    - (flux - flux_low)
                )
            speed_low, flux_low = speed, flux
        return flux_low

    def sweep_low(c):
        edge_flux[6 if c is None else c] = sweep_faces(c, 0, split_face, None, None)

    def sweep_high(c):
        sweep_faces(
            c,
            split_face,
            cells_x + 1,
            face_speed(split_face - 1),
            edge_flux[6 if c is None else c],
        )

    def low_step(c, carry):
        sweep_low(c)
        return carry

    def high_step(c, carry):
        sweep_high(c)
        return carry

    lax.fori_loop(0, 6, low_step, 0)
    sweep_low(None)
    halos[2].wait()
    halos[3].wait()
    sweep_high(None)
    for n in range(3):
        halos[4 + n].wait()
        lax.fori_loop(2 * n, 2 * n + 2, high_step, 0)

    def central_z(block):
        return 0.5 * (shift(block, 1, 2) - shift(block, -1, 2))

    def central_y(block, edge):
        ring = jnp.concatenate([block, edge], axis=1)
        return (0.5 * (shift(ring, 1, 1) - shift(ring, -1, 1)))[:, :cells_y]

    def central_x(ring):
        return 0.5 * (ring[2:] - ring[:-2])

    gradient = [
        [central_x(wide_vel(c)), central_y(vel[c], vel_side[c]), central_z(vel[c])]
        for c in range(3)
    ]
    old = [field[c] for c in range(6)]
    new = []
    for c in range(6):
        left_index, right_index = pair_list[c]
        stretch = None
        for inner in range(3):
            term = (
                gradient[left_index][inner] * old[slot_table[inner][right_index]]
                + old[slot_table[left_index][inner]] * gradient[right_index][inner]
            )
            stretch = term if stretch is None else stretch + term
        new.append(old[c] + time_step * (moved[c] + stretch))
        out_green[c] = new[c]
    new_fraction = field[6] + time_step * moved[6]
    out_frac[...] = new_fraction
    determinant = (
        new[0] * (new[1] * new[2] - new[5] * new[5])
        - new[3] * (new[3] * new[2] - new[5] * new[4])
        + new[4] * (new[3] * new[5] - new[1] * new[4])
    )
    dilate = dilation * (determinant - 1.0)
    scale = shear_modulus * new_fraction
    sigma = [scale * (new[c] - 1.0 + dilate) for c in range(3)]
    sigma += [scale * new[c] for c in range(3, 6)]
    xx, yy, zz, xy, xz, yz = sigma
    for n, part in enumerate((xx, xz, xy, yy, yz, zz)):
        stress[n] = part
    for n, part in enumerate((xy, yy, yz)):
        stress_pack[n] = fold(part)

    parts = (
        time_step * xx,
        2.0 * time_step * xy,
        vel[0] + 2.0 * time_step * central_z(xz),
        time_step * yy,
        vel[1] + 2.0 * time_step * central_z(yz),
        central_z(vel[2] + time_step * central_z(zz)),
    )
    stacked = jnp.concatenate(
        [part.reshape(cells_x * cells_y, length_z) for part in parts], axis=0
    )
    for copy in loads[3:]:
        copy.wait()
    modes_z = split_dot(table_z, split_values(stacked), ((1,), (1,)))
    modes_zy = split_dot(split_values(modes_z), send_table)
    for n in range(devices):
        outbox[n] = modes_zy[n * rows : (n + 1) * rows]

    if rungs:
        pl.semaphore_wait(rung_sem.at[len(rungs) - 1], 1)
    for target, device in others:
        remote(outbox.at[target], inbox.at[me], go_sem.at[0], go_sem.at[1], device).start()
    inbox[me] = outbox[me]
    stress_list = (
        (stress_pack, stress_side, over),
        (stress.at[:3, cells_x - 1 :], stress_low, right),
        (stress.at[:3, :1], stress_high, left),
    )
    edges = [
        remote(source, target, stress_sem.at[0, n], stress_sem.at[1, n], device)
        for n, (source, target, device) in enumerate(stress_list)
    ]
    for copy in edges:
        copy.start()

    norm = square_xy[...] + square_z[...][None]
    live = norm > 0.0
    total = float(count_x * cells_x * length_y * length_z)
    green_function = jnp.where(live, (-1.0 / total) / jnp.where(live, norm, 1.0), 0.0)
    green_function = green_function.reshape(-1, length_y)

    most = pl.ds(0, devices - 1)
    remote(outbox.at[most], inbox.at[most], go_sem.at[0], go_sem.at[1], right).wait()

    for n in range(count_x):
        held = inbox[n * count_y]
        for m in range(1, count_y):
            held = held + inbox[n * count_y + m]
        lines[n * rows : (n + 1) * rows] = held
    arranged = jnp.concatenate(
        [lines[:, n * length_y : (n + 1) * length_y] for n in range(wide)], axis=0
    )
    pressure_modes = split_values(split_dot(solve_in, split_values(arranged)) * green_function)
    turned = (
        narrow_dot(pressure_modes[0], turn_table[0])
        + narrow_dot(pressure_modes[0], turn_table[1])
        + narrow_dot(pressure_modes[1], turn_table[0])
    )
    pressure = split_dot(solve_out, split_values(turned))
    height = count_x * rows
    near_y = cells_y + 2
    for m in range(count_y):
        spread = jnp.concatenate(
            [
                pressure[n * height : (n + 1) * height, m * near_y : (m + 1) * near_y]
                for n in range(cells_x + 2)
            ]
            + [jnp.zeros((height, backbox.shape[2] - (cells_x + 2) * near_y), jnp.float32)],
            axis=1,
        )
        for n in range(count_x):
            backbox[n * count_y + m] = spread[n * rows : (n + 1) * rows]

    for target, device in others:
        remote(
            backbox.at[target], homebox.at[me], back_sem.at[0], back_sem.at[1], device
        ).start()
    homebox[me] = backbox[me]

    for copy in edges:
        copy.wait()
    force = (
        (0, 2, 0, 1),
        (2, 3, 1, 4),
        (1, 4, 2, 5),
    )
    for c, (part_x, part_y, edge_y, part_z) in enumerate(force):
        ring = jnp.concatenate([stress_low[part_x], stress[part_x], stress_high[part_x]], axis=0)
        pushed = (
            central_x(ring)
            + central_y(stress[part_y], stress_side[edge_y])
            + central_z(stress[part_z])
        )
        out_vel[c] = vel[c] + time_step * pushed

    remote(backbox.at[most], homebox.at[most], back_sem.at[0], back_sem.at[1], right).wait()
    for n in range(devices):
        final[n * rows : (n + 1) * rows] = homebox[n]


def finish_kernel(
    predicted,
    green,
    fraction,
    final,
    table_z,
    take_table,
    out_vel,
    out_green,
    out_frac,
    vel,
    sems,
):
    store_green = pltpu.make_async_copy(green, out_green, sems.at[0])
    store_frac = pltpu.make_async_copy(fraction, out_frac, sems.at[1])
    store_green.start()
    store_frac.start()
    taken = jnp.concatenate([take_table[...], take_table[...]], axis=1)
    slopes = narrow_dot(taken, jnp.concatenate(split_values(final[...]), axis=1), ((1,), (1,)))
    slopes = split_dot(split_values(slopes), table_z).reshape(predicted.shape)
    vel[0] = predicted[0] - slopes[0]
    vel[1] = predicted[1] - slopes[1]
    vel[2] = predicted[2] - 0.5 * (shift(slopes[2], 1, 2) - shift(slopes[2], -1, 2))
    store_vel = pltpu.make_async_copy(vel, out_vel, sems.at[2])
    store_vel.start()
    store_vel.wait()
    store_green.wait()
    store_frac.wait()


def fused_local(count_x, count_y, velocity, cauchy_green, labels):
    cells_x, cells_y, length_z = labels.shape
    devices = count_x * count_y
    rows = length_z // devices
    length_y = count_y * cells_y
    tables = spectral_tables(count_x, count_y, cells_x, cells_y, length_z)
    wide = (cells_x + 4) * length_y
    back = back_lanes(cells_x, cells_y)
    plane = (cells_y, length_z)
    real = functools.partial(pltpu.VMEM, dtype=jnp.float32)
    outputs = (
        jax.ShapeDtypeStruct(velocity.shape, jnp.float32),
        jax.ShapeDtypeStruct(cauchy_green.shape, jnp.float32),
        jax.ShapeDtypeStruct(labels.shape, jnp.float32),
    )
    handed = outputs + (
        jax.ShapeDtypeStruct((length_z, back), jnp.float32),
        jax.ShapeDtypeStruct(tables[0].shape, jnp.bfloat16),
        jax.ShapeDtypeStruct(tables[6].shape, jnp.bfloat16),
    )
    near = pl.BlockSpec(memory_space=pltpu.VMEM)
    far = pl.BlockSpec(memory_space=pltpu.HBM)
    scratch = [
        real(velocity.shape),
        real(cauchy_green.shape),
        pltpu.VMEM(labels.shape, jnp.int32),
        pltpu.VMEM(tables[1].shape[1:], jnp.bfloat16),
        pltpu.VMEM(tables[2].shape, jnp.bfloat16),
        pltpu.VMEM(tables[3].shape, jnp.bfloat16),
        real(tables[4].shape),
        real(tables[5].shape[1:]),
        pltpu.VMEM(tables[7].shape, jnp.bfloat16),
        real((7, cells_x) + plane),
        real((7, cells_x) + plane),
        real((7, cells_x, 8, length_z)),
        real((3, 2 * cells_x, length_z)),
        real((6, 3) + plane),
        real((6, 3) + plane),
        pltpu.VMEM((3,) + plane, jnp.int32),
        pltpu.VMEM((3,) + plane, jnp.int32),
        real((3, 1) + plane),
        real((3, 1) + plane),
        real((7, cells_x, 8, length_z)),
        real((3, 2 * cells_x, length_z)),
        real((3, cells_x, 8, length_z)),
        real((6, cells_x) + plane),
        real((3, cells_x, 8, length_z)),
        real((3, 1) + plane),
        real((3, 1) + plane),
        real((3, cells_x, 8, length_z)),
        real((devices, rows, wide)),
        real((devices, rows, wide)),
        real((count_x * rows, wide)),
        real((devices, rows, back)),
        real((devices, rows, back)),
        pltpu.SemaphoreType.DMA((11,)),
        pltpu.SemaphoreType.DMA((2, 10)),
        pltpu.SemaphoreType.DMA((2, 3)),
        pltpu.SemaphoreType.DMA((2,)),
        pltpu.SemaphoreType.DMA((2,)),
        pltpu.SemaphoreType.REGULAR((max(count_x.bit_length() - 1 - plane_bits, 1),)),
        real((7,) + plane),
    ]
    made = pl.pallas_call(
        functools.partial(step_kernel, count_x, count_y),
        out_shape=handed,
        in_specs=[far] * 11,
        out_specs=(near,) * 6,
        scratch_shapes=scratch,
        compiler_params=pltpu.CompilerParams(
            collective_id=0, has_side_effects=True, vmem_limit_bytes=32 * 1024 * 1024
        ),
        name="membrane_step",
    )(*[
        pltpu.with_memory_space_constraint(value, pltpu.HBM)
        for value in (velocity, cauchy_green, labels, *map(jnp.asarray, tables))
    ])
    return tuple(
        pl.pallas_call(
            finish_kernel,
            out_shape=outputs,
            in_specs=[near] * 6,
            out_specs=(far,) * 3,
            scratch_shapes=[real(velocity.shape), pltpu.SemaphoreType.DMA((3,))],
            compiler_params=pltpu.CompilerParams(vmem_limit_bytes=16 * 1024 * 1024),
            name="finish_step",
        )(*made)
    )


def fits_fused(count_x, count_y, shape):
    _, length_x, length_y, length_z = shape
    cells_x, cells_y = length_x // count_x, length_y // count_y
    devices = count_x * count_y
    return (
        count_y == 2
        and count_x > 2
        and count_x & (count_x - 1) == 0
        and length_z % 128 == 0
        and length_z % devices == 0
        and length_z // devices in (4, 8)
        and cells_x >= 4
        and cells_y % 8 == 0
        and cells_y >= 8
        and (cells_x + 4) * length_y % 128 == 0
        and length_x * length_y <= 4096
    )


def solution(mesh):
    placed = (P(None, "gx", "gy", None), P(None, "gx", "gy", None), P("gx", "gy", None))
    count_x, count_y = mesh.shape["gx"], mesh.shape["gy"]

    def step(velocity, cauchy_green, labels):
        if fits_fused(count_x, count_y, velocity.shape):
            body = functools.partial(fused_local, count_x, count_y)
        else:
            body = local
        return jax.shard_map(
            body, mesh=mesh, in_specs=placed, out_specs=placed, check_vma=False
        )(velocity, cauchy_green, labels)

    return step
```

```python
import functools
import math

import jax
import jax.numpy as jnp
import numpy as np
from jax import lax
from jax.experimental import pallas as pl
from jax.experimental.pallas import tpu as pltpu
from jax.sharding import PartitionSpec as P

time_step = 0.1
shear_modulus = 4.0
dilation = 0.5
weno_eps = 1e-06
pair_list = ((0, 0), (1, 1), (2, 2), (0, 1), (0, 2), (1, 2))
slot_table = ((0, 3, 4), (3, 1, 5), (4, 5, 2))
plane_bits = 2


def padded_2(block, sides, width):
    for axis, dim in sides:
        count = lax.axis_size(axis)
        forward = [(i, i + 1) for i in range(count - 1)]
        forward.append((count - 1, 0))
        backward = [(target, source) for source, target in forward]
        low = lax.ppermute(
            lax.slice_in_dim(block, block.shape[dim] - width, None, axis=dim), axis, forward
        )
        high = lax.ppermute(lax.slice_in_dim(block, 0, width, axis=dim), axis, backward)
        block = jnp.concatenate([low, block, high], axis=dim)
    return block


def weno_face(minus_two, minus_one, center, plus_one, plus_two):
    poly_zero = (2.0 * minus_two - 7.0 * minus_one + 11.0 * center) / 6.0
    poly_one = (-minus_one + 5.0 * center + 2.0 * plus_one) / 6.0
    poly_two = (2.0 * center + 5.0 * plus_one - plus_two) / 6.0
    curve_zero = minus_two - 2.0 * minus_one + center
    slope_zero = minus_two - 4.0 * minus_one + 3.0 * center
    curve_one = minus_one - 2.0 * center + plus_one
    slope_one = minus_one - plus_one
    curve_two = center - 2.0 * plus_one + plus_two
    slope_two = 3.0 * center - 4.0 * plus_one + plus_two
    smooth_zero = weno_eps + 13.0 / 12.0 * curve_zero * curve_zero + 0.25 * slope_zero * slope_zero
    smooth_one = weno_eps + 13.0 / 12.0 * curve_one * curve_one + 0.25 * slope_one * slope_one
    smooth_two = weno_eps + 13.0 / 12.0 * curve_two * curve_two + 0.25 * slope_two * slope_two
    weight_zero = 0.1 / (smooth_zero * smooth_zero)
    weight_one = 0.6 / (smooth_one * smooth_one)
    weight_two = 0.3 / (smooth_two * smooth_two)
    return (weight_zero * poly_zero + weight_one * poly_one + weight_two * poly_two) / (
        weight_zero + weight_one + weight_two
    )


def face_flux(shifted, speed_face):
    upwind_left = weno_face(shifted(-2), shifted(-1), shifted(0), shifted(1), shifted(2))
    upwind_right = weno_face(shifted(3), shifted(2), shifted(1), shifted(0), shifted(-1))
    return speed_face * jnp.where(speed_face >= 0.0, upwind_left, upwind_right)


def sweep(quantity, advecting, sweep_dim, anchor, count):

    def shifted(offset):
        return lax.slice_in_dim(
            quantity, anchor - 1 + offset, anchor + offset + count, axis=sweep_dim
        )

    speed_face = 0.5 * (
        lax.slice_in_dim(advecting, anchor - 1, anchor + count, axis=sweep_dim - 1)
        + lax.slice_in_dim(advecting, anchor, anchor + count + 1, axis=sweep_dim - 1)
    )
    flux_face = face_flux(shifted, speed_face)
    flux_upper = lax.slice_in_dim(flux_face, 1, count + 1, axis=sweep_dim)
    flux_lower = lax.slice_in_dim(flux_face, 0, count, axis=sweep_dim)
    center = lax.slice_in_dim(quantity, anchor, anchor + count, axis=sweep_dim)
    spread = lax.slice_in_dim(speed_face, 1, count + 1, axis=sweep_dim - 1) - lax.slice_in_dim(
        speed_face, 0, count, axis=sweep_dim - 1
    )
    return center * spread - (flux_upper - flux_lower)


def sweep_periodic(quantity, advecting):

    def shifted(offset):
        return jnp.roll(quantity, -offset, 3)

    speed_face = 0.5 * (advecting + jnp.roll(advecting, -1, 2))
    flux_face = face_flux(shifted, speed_face)
    return quantity * (speed_face - jnp.roll(speed_face, 1, 2)) - (
        flux_face - jnp.roll(flux_face, 1, 3)
    )


def region_gradient(padded, anchor, count_x, count_y):
    gradient = []
    for component in range(3):
        advecting = padded[7 + component]
        center = advecting[anchor : anchor + count_x, anchor : anchor + count_y]
        along_x = 0.5 * (
            advecting[anchor + 1 : anchor + 1 + count_x, anchor : anchor + count_y]
            - advecting[anchor - 1 : anchor - 1 + count_x, anchor : anchor + count_y]
        )
        along_y = 0.5 * (
            advecting[anchor : anchor + count_x, anchor + 1 : anchor + 1 + count_y]
            - advecting[anchor : anchor + count_x, anchor - 1 : anchor - 1 + count_y]
        )
        along_z = 0.5 * (jnp.roll(center, -1, 2) - jnp.roll(center, 1, 2))
        gradient.append([along_x, along_y, along_z])
    return gradient


def advance(green, fraction, transported, gradient):
    updated = []
    for component in range(6):
        left_index, right_index = pair_list[component]
        stretch = jnp.zeros_like(green[0])
        for inner_index in range(3):
            stretch = (
                stretch
                + gradient[left_index][inner_index] * green[slot_table[inner_index][right_index]]
            )
            stretch = (
                stretch
                + green[slot_table[left_index][inner_index]] * gradient[right_index][inner_index]
            )
        updated.append(green[component] + time_step * (transported[component] + stretch))
    return (jnp.stack(updated), fraction + time_step * transported[6])


def membrane_stress(green, fraction):
    determinant = (
        green[0] * (green[1] * green[2] - green[5] * green[5])
        - green[3] * (green[3] * green[2] - green[5] * green[4])
        + green[4] * (green[3] * green[5] - green[1] * green[4])
    )
    dilate = dilation * (determinant - 1.0)
    stress_parts = []
    for component in range(6):
        if component < 3:
            stress_parts.append(green[component] - 1.0 + dilate)
        else:
            stress_parts.append(green[component])
    return shear_modulus * fraction * jnp.stack(stress_parts)


def update_region(padded, anchor, count_x, count_y):
    carried = padded[:7]
    transported = sweep(
        carried[:, :, anchor : anchor + count_y],
        padded[7, :, anchor : anchor + count_y],
        1,
        anchor,
        count_x,
    )
    transported = transported + sweep(
        carried[:, anchor : anchor + count_x],
        padded[8, anchor : anchor + count_x],
        2,
        anchor,
        count_y,
    )
    region = padded[:, anchor : anchor + count_x, anchor : anchor + count_y]
    transported = transported + sweep_periodic(region[:7], region[9])
    gradient = region_gradient(padded, anchor, count_x, count_y)
    new_green, new_fraction = advance(region[:6], region[6], transported, gradient)
    return (new_green, new_fraction, membrane_stress(new_green, new_fraction))


def derive_x(widened):
    return 0.5 * (widened[..., 2:, 1:-1, :] - widened[..., :-2, 1:-1, :])


def derive_y(widened):
    return 0.5 * (widened[..., 1:-1, 2:, :] - widened[..., 1:-1, :-2, :])


def derive_z(widened):
    inside = widened[..., 1:-1, 1:-1, :]
    return 0.5 * (jnp.roll(inside, -1, -1) - jnp.roll(inside, 1, -1))


def stress_force(widened):
    return jnp.stack(
        [
            derive_x(widened[slot_table[index_row][0]])
            + derive_y(widened[slot_table[index_row][1]])
            + derive_z(widened[slot_table[index_row][2]])
            for index_row in range(3)
        ]
    )


def dft_tables(length):
    wave_index = jnp.arange(length, dtype=jnp.int32)
    phase_index = wave_index[:, None] * wave_index[None, :] % length
    angle_table = 2.0 * math.pi / length * phase_index.astype(jnp.float32)
    return (jnp.cos(angle_table), jnp.sin(angle_table))


def contract(einsum_form, values, dft_table):
    return jnp.einsum(einsum_form, values, dft_table, precision=lax.Precision.HIGHEST)


def forward_transform(cell_field):
    components, cells_x, cells_y, length_z = cell_field.shape
    length_x = cells_x * lax.axis_size("gx")
    length_y = cells_y * lax.axis_size("gy")
    slab_z = length_z // lax.axis_size("gx")
    cosine_z, sine_z = dft_tables(length_z)
    real_z = contract("cxyz,zk->cxyk", cell_field, cosine_z)
    imag_z = -contract("cxyz,zk->cxyk", cell_field, sine_z)
    lines_x = lax.all_to_all(
        jnp.stack([real_z, imag_z], 1), "gx", split_axis=4, concat_axis=2, tiled=True
    )
    lines_x = lines_x.reshape(components, 2, length_x, cells_y * slab_z)
    cosine_x, sine_x = dft_tables(length_x)
    real_part = lines_x[:, 0]
    imag_part = lines_x[:, 1]
    real_x = contract("cxm,xk->ckm", real_part, cosine_x) + contract(
        "cxm,xk->ckm", imag_part, sine_x
    )
    imag_x = contract("cxm,xk->ckm", imag_part, cosine_x) - contract(
        "cxm,xk->ckm", real_part, sine_x
    )
    paired_x = jnp.stack([real_x, imag_x], 1).reshape(components, 2, length_x, cells_y, slab_z)
    lines_y = lax.all_to_all(paired_x, "gy", split_axis=2, concat_axis=3, tiled=True)
    cosine_y, sine_y = dft_tables(length_y)
    real_part = lines_y[:, 0]
    imag_part = lines_y[:, 1]
    real_y = contract("cayz,yk->ckaz", real_part, cosine_y) + contract(
        "cayz,yk->ckaz", imag_part, sine_y
    )
    imag_y = contract("cayz,yk->ckaz", imag_part, cosine_y) - contract(
        "cayz,yk->ckaz", real_part, sine_y
    )
    return (real_y, imag_y)


def inverse_transform(real_k, imag_k, cells_y, length_z):
    components, length_y, block_x, slab_z = real_k.shape
    length_x = block_x * lax.axis_size("gy")
    cosine_y, sine_y = dft_tables(length_y)
    real_y = contract("ckaz,ky->cayz", real_k, cosine_y) - contract("ckaz,ky->cayz", imag_k, sine_y)
    imag_y = contract("ckaz,ky->cayz", real_k, sine_y) + contract("ckaz,ky->cayz", imag_k, cosine_y)
    lines_x = lax.all_to_all(
        jnp.stack([real_y, imag_y], 1), "gy", split_axis=3, concat_axis=2, tiled=True
    )
    lines_x = lines_x.reshape(components, 2, length_x, cells_y * slab_z)
    cosine_x, sine_x = dft_tables(length_x)
    real_part = lines_x[:, 0]
    imag_part = lines_x[:, 1]
    real_x = contract("ckm,kx->cxm", real_part, cosine_x) - contract(
        "ckm,kx->cxm", imag_part, sine_x
    )
    imag_x = contract("ckm,kx->cxm", real_part, sine_x) + contract(
        "ckm,kx->cxm", imag_part, cosine_x
    )
    paired_x = jnp.stack([real_x, imag_x], 1).reshape(components, 2, length_x, cells_y, slab_z)
    slab_pairs = lax.all_to_all(paired_x, "gx", split_axis=2, concat_axis=4, tiled=True)
    cosine_z, sine_z = dft_tables(length_z)
    result = contract("cxyk,kz->cxyz", slab_pairs[:, 0], cosine_z) - contract(
        "cxyk,kz->cxyz", slab_pairs[:, 1], sine_z
    )
    return result / float(length_x * length_y * length_z)


def sine_numbers(wave_index, length):
    silent = wave_index % (length // 2) == 0
    sine_value = jnp.sin(2.0 * math.pi / length * wave_index.astype(jnp.float32))
    return (jnp.where(silent, 0.0, sine_value), silent)


def wave_numbers(length_y, block_x, slab_z, length_x, length_z):
    index_y = jnp.arange(length_y, dtype=jnp.int32)
    index_x = lax.axis_index("gy") * block_x + jnp.arange(block_x, dtype=jnp.int32)
    index_z = lax.axis_index("gx") * slab_z + jnp.arange(slab_z, dtype=jnp.int32)
    sine_x, silent_x = sine_numbers(index_x, length_x)
    sine_y, silent_y = sine_numbers(index_y, length_y)
    sine_z, silent_z = sine_numbers(index_z, length_z)
    live_mode = jnp.logical_not(
        silent_y[:, None, None] & silent_x[None, :, None] & silent_z[None, None, :]
    )
    return ((sine_x[None, :, None], sine_y[:, None, None], sine_z[None, None, :]), live_mode)


def local(velocity, cauchy_green, labels):
    cells_x = velocity.shape[1]
    cells_y = velocity.shape[2]
    length_z = velocity.shape[3]
    fraction = labels.astype(jnp.float32) * 0.25
    stacked = jnp.concatenate([cauchy_green, fraction[None], velocity], 0)
    padded = padded_2(stacked, (("gx", 1), ("gy", 2)), 4)
    green_wide, fraction_wide, stress_wide = update_region(padded, 3, cells_x + 2, cells_y + 2)
    new_green = green_wide[:, 1:-1, 1:-1]
    new_fraction = fraction_wide[1:-1, 1:-1]
    predicted = velocity + time_step * stress_force(stress_wide)
    length_x = cells_x * lax.axis_size("gx")
    velocity_wide = padded_2(predicted, (("gx", 1), ("gy", 2)), 1)
    divergence = (
        derive_x(velocity_wide[0]) + derive_y(velocity_wide[1]) + derive_z(velocity_wide[2])
    )
    real_k, imag_k = forward_transform(divergence[None])
    sine_list, live_mode = wave_numbers(
        real_k.shape[1], real_k.shape[2], real_k.shape[3], length_x, length_z
    )
    norm_sq = (
        sine_list[0] * sine_list[0] + sine_list[1] * sine_list[1] + sine_list[2] * sine_list[2]
    )
    safe_norm = jnp.where(live_mode, norm_sq, 1.0)
    pressure_real = jnp.where(live_mode, -real_k[0] / safe_norm, 0.0)
    pressure_imag = jnp.where(live_mode, -imag_k[0] / safe_norm, 0.0)
    pressure = inverse_transform(pressure_real[None], pressure_imag[None], cells_y, length_z)
    pressure_wide = padded_2(pressure, (("gx", 1), ("gy", 2)), 1)
    new_velocity = predicted - jnp.stack(
        [derive_x(pressure_wide[0]), derive_y(pressure_wide[0]), derive_z(pressure_wide[0])]
    )
    return (new_velocity, new_green, new_fraction)


def hartley(length):
    index = np.arange(length)
    angle = 2.0 * np.pi / length * (np.outer(index, index) % length)
    return np.cos(angle) + np.sin(angle)


def sine_squares(length):
    index = np.arange(length)
    sine = np.where(index % (length // 2) == 0, 0.0, np.sin(2.0 * np.pi / length * index))
    return sine * sine


def split_table(table):
    high = np.asarray(table, jnp.bfloat16)
    low = np.asarray(table - np.asarray(high, np.float64), jnp.bfloat16)
    return np.stack([high, low])


def back_lanes(cells_x, cells_y):
    return -(-(cells_x + 2) * (cells_y + 2) // 128) * 128


def spectral_tables(count_x, count_y, cells_x, cells_y, length_z):
    length_x, length_y = count_x * cells_x, count_y * cells_y
    devices = count_x * count_y
    rows = length_z // devices
    table_x, table_y, table_z = hartley(length_x), hartley(length_y), hartley(length_z)
    wide = cells_x + 4
    stencils = (
        {0: 1.0},
        {-1: 0.5, 1: -0.5},
        {-2: 0.25, 0: -0.5, 2: 0.25},
    )
    field_orders = ((2, 0), (1, 1), (1, 0), (0, 2), (0, 1), (0, 0))
    lanes = wide * cells_y
    send_table = np.zeros((6, cells_x, cells_y, lanes + 128))
    outside = {}
    for field, (order_x, order_y) in enumerate(field_orders):
        for x, y in np.ndindex(cells_x, cells_y):
            for offset_x, weight_x in stencils[order_x].items():
                for offset_y, weight_y in stencils[order_y].items():
                    column, line = x + 2 + offset_x, y + offset_y
                    target = send_table[field, x, y]
                    if 0 <= line < cells_y:
                        target[column * cells_y + line] += weight_x * weight_y
                    else:
                        spot = outside.setdefault((column, line), len(outside))
                        target[lanes + spot :: 128 // rows] += weight_x * weight_y
    spread_table = np.zeros((count_y, 2, lanes, wide, length_y))
    for block in range(count_y):
        for column, line in np.ndindex(wide, cells_y):
            place = block * cells_y + line
            spread_table[block, 0, column * cells_y + line, column] = table_y[place]
        for (column, line), spot in outside.items():
            place = (block * cells_y + line) % length_y
            spread_table[block, 1, spot :: 128 // rows, column] = table_y[place]
    spread_table = np.moveaxis(spread_table, 0, 1)
    near_x, near_y = cells_x + 2, cells_y + 2
    take_table = np.zeros((3, cells_x, cells_y, back_lanes(cells_x, cells_y)))
    turn_table = np.zeros((length_y, count_y, near_y))
    for block in range(count_y):
        ring = (block * cells_y + np.arange(near_y) - 1) % length_y
        turn_table[:, block] = table_y[:, ring]
    for x in range(cells_x):
        for y in range(cells_y):
            place = (x + 1) * near_y + y + 1
            take_table[0, x, y, place + near_y] = 0.5
            take_table[0, x, y, place - near_y] = -0.5
            take_table[1, x, y, place + 1] = 0.5
            take_table[1, x, y, place - 1] = -0.5
            take_table[2, x, y, place] = 1.0
    same = np.eye(rows)
    reach = (
        np.arange(count_x)[None, :] * cells_x + np.arange(wide)[:, None] - 2
    ) % length_x
    solve_in = np.einsum("kib,qr->kqibr", table_x[:, reach], same).reshape(
        length_x * rows, wide * count_x * rows
    )
    home = np.arange(count_x)[None, :] * cells_x + np.arange(near_x)[:, None] - 1
    solve_out = np.einsum("ibk,qr->ibqkr", table_x[home % length_x], same).reshape(
        near_x * count_x * rows, length_x * rows
    )
    square_xy = np.repeat(sine_squares(length_x), rows)[:, None] + sine_squares(length_y)[None, :]
    square_z = sine_squares(length_z).reshape(devices, rows)
    square_z = np.tile(square_z, (1, 8 // rows))[:, :, None] * np.ones((1, 1, length_y))
    send_table = send_table.reshape(6 * cells_x * cells_y, lanes + 128)
    spread_table = spread_table.reshape(-1, wide * length_y)
    take_table = take_table.reshape(3 * cells_x * cells_y, -1)
    return (
        split_table(table_z),
        np.asarray(send_table, jnp.bfloat16),
        split_table(solve_in),
        split_table(solve_out),
        np.asarray(square_xy.reshape(-1, 8, length_y), np.float32),
        np.asarray(square_z, np.float32),
        np.asarray(take_table, jnp.bfloat16),
        split_table(turn_table.reshape(length_y, count_y * near_y)),
        split_table(spread_table),
    )


def shift(values, offset, axis):
    extent = values.shape[axis]
    if offset % extent == 0:
        return values
    return pltpu.roll(values, (-offset) % extent, axis)


def weno_one(a, b, c, d, e):
    poly_zero = 2.0 * a - 7.0 * b + 11.0 * c
    poly_one = 5.0 * c - b + 2.0 * d
    poly_two = 2.0 * c + 5.0 * d - e
    curve_zero = a - 2.0 * b + c
    slope_zero = a - 4.0 * b + 3.0 * c
    curve_one = b - 2.0 * c + d
    slope_one = b - d
    curve_two = c - 2.0 * d + e
    slope_two = 3.0 * c - 4.0 * d + e
    big = 13.0 / 12.0
    smooth_zero = weno_eps + big * curve_zero * curve_zero + 0.25 * slope_zero * slope_zero
    smooth_one = weno_eps + big * curve_one * curve_one + 0.25 * slope_one * slope_one
    smooth_two = weno_eps + big * curve_two * curve_two + 0.25 * slope_two * slope_two
    zero_one = smooth_zero * smooth_one
    zero_two = smooth_zero * smooth_two
    one_two = smooth_one * smooth_two
    weight_zero = one_two * one_two
    weight_one = 6.0 * (zero_two * zero_two)
    weight_two = 3.0 * (zero_one * zero_one)
    return (weight_zero * poly_zero + weight_one * poly_one + weight_two * poly_two) / (
        6.0 * (weight_zero + weight_one + weight_two)
    )


def upwind_flux(at, speed):
    positive = speed >= 0.0
    minus_two, minus_one, center, one, two, three = [at(o) for o in range(-2, 4)]
    pick = functools.partial(jnp.where, positive)
    return speed * weno_one(
        pick(minus_two, three),
        pick(minus_one, two),
        pick(center, one),
        pick(one, center),
        pick(two, minus_one),
    )


def ring_sweep(values, advecting, axis):
    speed = 0.5 * (advecting + shift(advecting, 1, axis))
    flux = upwind_flux(lambda o: shift(values, o, axis), speed)
    return values * (speed - shift(speed, -1, axis)) - (flux - shift(flux, -1, axis))


def split_values(values):
    high = values.astype(jnp.bfloat16)
    return high, (values - high.astype(jnp.float32)).astype(jnp.bfloat16)


def narrow_dot(left, right, dims=((1,), (0,))):
    return lax.dot_general(
        left, right, (dims, ((), ())), preferred_element_type=jnp.float32
    )


def split_dot(left, right, dims=((1,), (0,))):
    joined_left = jnp.concatenate([left[0], left[0], left[1]], axis=dims[0][0])
    joined_right = jnp.concatenate([right[0], right[1], right[0]], axis=dims[1][0])
    return narrow_dot(joined_left, joined_right, dims)


def step_kernel(
    count_x,
    count_y,
    vel_far,
    green_far,
    labels_far,
    table_z_far,
    send_table_far,
    solve_in_far,
    solve_out_far,
    square_xy_far,
    square_z_far,
    take_table_far,
    turn_table_far,
    spread_table_far,
    out_vel,
    out_green,
    out_frac,
    final,
    table_z,
    take_table,
    vel,
    green,
    labels,
    send_table,
    solve_in,
    solve_out,
    square_xy,
    square_z,
    turn_table,
    spread_table,
    field,
    moved,
    pack,
    vel_pack,
    low_wide,
    high_wide,
    low_label,
    high_label,
    low_vel,
    high_vel,
    side,
    vel_near,
    vel_side,
    stress,
    stress_pack,
    stress_low,
    stress_high,
    stress_side,
    outbox,
    inbox,
    backbox,
    homebox,
    load_sem,
    halo_sem,
    stress_sem,
    go_sem,
    back_sem,
    rung_sem,
    edge_flux,
):
    cells_x, cells_y, length_z = labels.shape
    devices = count_x * count_y
    rows = length_z // devices
    length_y = count_y * cells_y
    wide = cells_x + 4
    lanes = wide * cells_y
    me_x = lax.axis_index("gx")
    me_y = lax.axis_index("gy")
    me = me_x * count_y + me_y
    mesh_type = pl.DeviceIdType.MESH

    turns = []
    for bit in range(count_x.bit_length() - 1):
        weight = 1 << bit
        turns.append(weight * (1 - 2 * lax.rem(me_x // weight, 2)))
    others = []
    for step in range(devices - 1, 0, -1):
        peer_x, peer_y = me_x, me_y
        for bit, turn in enumerate(turns):
            if (step // count_y) >> bit & 1:
                peer_x = peer_x + turn
        if step % count_y:
            peer_y = 1 - me_y
        others.append((peer_x * count_y + peer_y, (peer_x, peer_y)))

    def toggled(mask, flip):
        place = me_x
        for bit, turn in enumerate(turns):
            if mask >> bit & 1:
                place = place + turn
        return (place, 1 - me_y if flip else me_y)

    right = (lax.rem(me_x + 1, count_x), me_y)
    left = (lax.rem(me_x + count_x - 1, count_x), me_y)
    over = (me_x, 1 - me_y)
    rungs = [toggled(1 << bit, False) for bit in range(plane_bits, len(turns))]
    mates = [toggled(mask, flip) for mask in range(1 << plane_bits) for flip in (0, 1)][1:]
    greeted = [left, right] + rungs + mates
    barrier = pltpu.get_barrier_semaphore()
    for device in greeted:
        pl.semaphore_signal(barrier, inc=1, device_id=device, device_id_type=mesh_type)

    load_list = (
        (vel_far, vel),
        (green_far, green),
        (labels_far, labels),
        (table_z_far, table_z),
        (send_table_far, send_table),
        (square_xy_far, square_xy),
        (square_z_far.at[me], square_z),
        (solve_in_far, solve_in),
        (solve_out_far, solve_out),
        (take_table_far, take_table),
        (turn_table_far, turn_table),
        (spread_table_far, spread_table),
    )
    loads = [
        pltpu.make_async_copy(source, target, load_sem.at[n])
        for n, (source, target) in enumerate(load_list)
    ]
    for copy in loads:
        copy.start()
    for copy in loads[:3]:
        copy.wait()

    fraction = labels[...].astype(jnp.float32) * 0.25
    for c in range(6):
        field[c] = green[c]
    field[6] = fraction
    row = lax.broadcasted_iota(jnp.int32, (cells_x, 8, length_z), 1)

    def fold(values):
        return jnp.where(row < 4, values[:, :8], values[:, cells_y - 8 :])

    for c in range(7):
        pack[c] = fold(field[c])
    for c in range(3):
        for x in range(cells_x):
            vel_pack[c, 2 * x] = vel[c, x, 0]
            vel_pack[c, 2 * x + 1] = vel[c, x, cells_y - 1]
            vel_side[c, x] = jnp.zeros((8, length_z), jnp.float32)

    def sweep_z(c, carry):
        for x in range(cells_x):
            moved[c, x] = ring_sweep(field[c, x], vel[2, x], 1)
        return carry

    @pl.when(me_x == 0)
    def _():
        lax.fori_loop(0, 7, sweep_z, 0)

    pl.semaphore_wait(barrier, len(greeted))


    def remote(source, target, send_sem, recv_sem, device):
        return pltpu.make_async_remote_copy(
            src_ref=source,
            dst_ref=target,
            send_sem=send_sem,
            recv_sem=recv_sem,
            device_id=device,
            device_id_type=mesh_type,
        )

    y_pieces = ((0, 3), (3, 5), (5, 7))
    x_pieces = ((0, 2), (2, 4), (4, 6))
    halo_list = (
        (vel_pack, vel_near, over),
        *[
            (pack.at[first:last], side.at[first:last], over)
            for first, last in y_pieces
        ],
        (vel.at[:, :1], high_vel, left),
        (labels.at[:3], high_label, left),
        *[
            (green.at[first:last, :3], high_wide.at[first:last], left)
            for first, last in x_pieces
        ],
        (vel.at[:, cells_x - 1 :], low_vel, right),
        (labels.at[cells_x - 3 :], low_label, right),
        *[
            (green.at[first:last, cells_x - 3 :], low_wide.at[first:last], right)
            for first, last in x_pieces
        ],
    )
    halos = [
        remote(source, target, halo_sem.at[0, n], halo_sem.at[1, n], device)
        for n, (source, target, device) in enumerate(halo_list)
    ]
    for copy in halos:
        copy.start()
    y_halos, high_halos, low_halos = halos[1:4], halos[4:9], halos[9:14]

    def tell(n):
        pl.semaphore_signal(rung_sem.at[n], inc=1, device_id=rungs[n], device_id_type=mesh_type)

    if rungs:
        tell(0)

    @pl.when(me_x != 0)
    def _():
        lax.fori_loop(0, 7, sweep_z, 0)

    halos[0].wait()
    for c in range(3):
        for x in range(cells_x):
            vel_side[c, x, 0] = vel_near[c, 2 * x]
            vel_side[c, x, 7] = vel_near[c, 2 * x + 1]
    for n in range(1, len(rungs)):
        pl.semaphore_wait(rung_sem.at[n - 1], 1)
        tell(n)
    def sweep_y(c, carry):
        for x in range(cells_x):
            values = jnp.concatenate([field[c, x], side[c, x]], axis=0)
            advecting = jnp.concatenate([vel[1, x], vel_side[1, x]], axis=0)
            moved[c, x] = moved[c, x] + ring_sweep(values, advecting, 0)[:cells_y]
        return carry

    for copy, (first, last) in zip(y_halos, y_pieces):
        copy.wait()
        lax.fori_loop(first, last, sweep_y, 0)

    def face_speed(face):
        before = low_vel[0, 0] if face == 0 else vel[0, face - 1]
        after = high_vel[0, 0] if face == cells_x else vel[0, face]
        return 0.5 * (before + after)

    def plane_at(c, n):
        if n < 3:
            return low_wide[c, n]
        if n < cells_x + 3:
            return field[c, n - 3]
        return high_wide[c, n - cells_x - 3]

    def settle(c, x, speeds, fluxes):
        moved[c, x] = (
            moved[c, x]
            + plane_at(c, x + 3) * (speeds[1] - speeds[0])
            - (fluxes[1] - fluxes[0])
        )

    def sweep_faces(c, first, last):
        before = None
        opening = None
        for face in range(first, last):
            speed = face_speed(face)
            flux = upwind_flux(lambda o: plane_at(c, face + 2 + o), speed)
            if before is None:
                opening = (speed, flux)
            else:
                settle(c, face - 1, (before[0], speed), (before[1], flux))
            before = (speed, flux)
        return opening, before

    def low_first(c, carry):
        edge_flux[c] = sweep_faces(c, 0, middle)[1][1]
        return carry

    def high_last(c, carry):
        opening, _ = sweep_faces(c, middle, cells_x + 1)
        speed = face_speed(middle - 1)
        settle(c, middle - 1, (speed, opening[0]), (edge_flux[c], opening[1]))
        return carry

    def high_first(c, carry):
        edge_flux[c] = sweep_faces(c, middle + 1, cells_x + 1)[0][1]
        return carry

    def low_last(c, carry):
        _, closing = sweep_faces(c, 0, middle + 1)
        speed = face_speed(middle + 1)
        settle(c, middle, (closing[0], speed), (closing[1], edge_flux[c]))
        return carry

    middle = cells_x - 2

    def take_low(step):
        low_halos[0].wait()
        low_halos[1].wait()
        low_wide[6] = low_label[...].astype(jnp.float32) * 0.25
        lax.fori_loop(6, 7, step, 0)
        for copy, (first, last) in zip(low_halos[2:], x_pieces):
            copy.wait()
            lax.fori_loop(first, last, step, 0)

    def take_high(step):
        high_halos[0].wait()
        high_halos[1].wait()
        high_wide[6] = high_label[...].astype(jnp.float32) * 0.25
        lax.fori_loop(6, 7, step, 0)
        for copy, (first, last) in zip(high_halos[2:], x_pieces):
            copy.wait()
            lax.fori_loop(first, last, step, 0)

    odd = lax.rem(me_x, 2) == 1

    @pl.when(odd)
    def _():
        take_low(low_first)
        take_high(high_last)

    @pl.when(jnp.logical_not(odd))
    def _():
        take_high(high_first)
        take_low(low_last)

    def wide_vel(c):
        return jnp.concatenate([low_vel[c], vel[c], high_vel[c]], axis=0)

    def central_z(block):
        return 0.5 * (shift(block, 1, 2) - shift(block, -1, 2))

    def central_y(block, edge):
        ring = jnp.concatenate([block, edge], axis=1)
        return (0.5 * (shift(ring, 1, 1) - shift(ring, -1, 1)))[:, :cells_y]

    def central_x(ring):
        return 0.5 * (ring[2:] - ring[:-2])

    gradient = [
        [central_x(wide_vel(c)), central_y(vel[c], vel_side[c]), central_z(vel[c])]
        for c in range(3)
    ]
    old = [field[c] for c in range(6)]
    new = []
    for c in range(6):
        left_index, right_index = pair_list[c]
        stretch = None
        for inner in range(3):
            term = (
                gradient[left_index][inner] * old[slot_table[inner][right_index]]
                + old[slot_table[left_index][inner]] * gradient[right_index][inner]
            )
            stretch = term if stretch is None else stretch + term
        new.append(old[c] + time_step * (moved[c] + stretch))
        out_green[c] = new[c]
    new_fraction = field[6] + time_step * moved[6]
    out_frac[...] = new_fraction
    determinant = (
        new[0] * (new[1] * new[2] - new[5] * new[5])
        - new[3] * (new[3] * new[2] - new[5] * new[4])
        + new[4] * (new[3] * new[5] - new[1] * new[4])
    )
    dilate = dilation * (determinant - 1.0)
    scale = shear_modulus * new_fraction
    sigma = [scale * (new[c] - 1.0 + dilate) for c in range(3)]
    sigma += [scale * new[c] for c in range(3, 6)]
    xx, yy, zz, xy, xz, yz = sigma
    for n, part in enumerate((xx, xz, xy, yy, yz, zz)):
        stress[n] = part
    for n, part in enumerate((xy, yy, yz)):
        stress_pack[n] = fold(part)

    parts = (
        time_step * xx,
        2.0 * time_step * xy,
        vel[0] + 2.0 * time_step * central_z(xz),
        time_step * yy,
        vel[1] + 2.0 * time_step * central_z(yz),
        central_z(vel[2] + time_step * central_z(zz)),
    )
    stacked = jnp.concatenate(
        [part.reshape(cells_x * cells_y, length_z) for part in parts], axis=0
    )
    def own_slot(values):
        row_slot = lax.rem(lax.broadcasted_iota(jnp.int32, values.shape, 0), rows)
        lane_slot = lax.broadcasted_iota(jnp.int32, values.shape, 1) // (128 // rows)
        return jnp.where(row_slot == lane_slot, values, 0.0)

    for copy in loads[3:]:
        copy.wait()
    modes_z = split_dot(table_z, split_values(stacked), ((1,), (1,)))
    weights = send_table[...]
    sent = narrow_dot(
        jnp.concatenate(split_values(modes_z), axis=1), jnp.concatenate([weights, weights], axis=0)
    )
    fringe = own_slot(sent[:, lanes:])
    fringe = fringe + shift(fringe, 1, 0)
    fringe = fringe + shift(fringe, 2, 0)
    for n in range(devices):
        outbox[n, :rows] = sent[n * rows : (n + 1) * rows, :lanes]
        outbox[n, rows] = fringe[n * rows]

    if rungs:
        pl.semaphore_wait(rung_sem.at[len(rungs) - 1], 1)
    for target, device in others:
        remote(outbox.at[target], inbox.at[me], go_sem.at[0], go_sem.at[1], device).start()
    inbox[me] = outbox[me]
    stress_list = (
        (stress_pack, stress_side, over),
        (stress.at[:3, cells_x - 1 :], stress_low, right),
        (stress.at[:3, :1], stress_high, left),
    )
    edges = [
        remote(source, target, stress_sem.at[0, n], stress_sem.at[1, n], device)
        for n, (source, target, device) in enumerate(stress_list)
    ]
    for copy in edges:
        copy.start()

    norm = square_xy[...] + square_z[...][None]
    live = norm > 0.0
    total = float(count_x * cells_x * length_y * length_z)
    green_function = jnp.where(live, (-1.0 / total) / jnp.where(live, norm, 1.0), 0.0)
    green_function = green_function.reshape(-1, length_y)

    most = pl.ds(0, devices - 1)
    remote(outbox.at[most], inbox.at[most], go_sem.at[0], go_sem.at[1], right).wait()

    blocks = [
        jnp.concatenate([inbox[n * count_y + m, :rows] for n in range(count_x)], axis=0)
        for m in range(count_y)
    ]
    for m in range(count_y):
        fringe = [
            jnp.broadcast_to(inbox[n * count_y + m, rows:], (rows, lanes)) for n in range(count_x)
        ]
        blocks.append(own_slot(jnp.concatenate(fringe, axis=0)))
    lines = split_dot(split_values(jnp.concatenate(blocks, axis=1)), spread_table)
    arranged = jnp.concatenate(
        [lines[:, n * length_y : (n + 1) * length_y] for n in range(wide)], axis=0
    )
    pressure_modes = split_values(split_dot(solve_in, split_values(arranged)) * green_function)
    turned = (
        narrow_dot(pressure_modes[0], turn_table[0])
        + narrow_dot(pressure_modes[0], turn_table[1])
        + narrow_dot(pressure_modes[1], turn_table[0])
    )
    pressure = split_dot(solve_out, split_values(turned))
    height = count_x * rows
    near_y = cells_y + 2
    for m in range(count_y):
        spread = jnp.concatenate(
            [
                pressure[n * height : (n + 1) * height, m * near_y : (m + 1) * near_y]
                for n in range(cells_x + 2)
            ]
            + [jnp.zeros((height, backbox.shape[2] - (cells_x + 2) * near_y), jnp.float32)],
            axis=1,
        )
        for n in range(count_x):
            backbox[n * count_y + m] = spread[n * rows : (n + 1) * rows]

    for target, device in others:
        remote(
            backbox.at[target], homebox.at[me], back_sem.at[0], back_sem.at[1], device
        ).start()
    homebox[me] = backbox[me]

    for copy in edges:
        copy.wait()
    force = (
        (0, 2, 0, 1),
        (2, 3, 1, 4),
        (1, 4, 2, 5),
    )
    for c, (part_x, part_y, edge_y, part_z) in enumerate(force):
        ring = jnp.concatenate([stress_low[part_x], stress[part_x], stress_high[part_x]], axis=0)
        pushed = (
            central_x(ring)
            + central_y(stress[part_y], stress_side[edge_y])
            + central_z(stress[part_z])
        )
        out_vel[c] = vel[c] + time_step * pushed

    remote(backbox.at[most], homebox.at[most], back_sem.at[0], back_sem.at[1], right).wait()
    for n in range(devices):
        final[n * rows : (n + 1) * rows] = homebox[n]


def finish_kernel(
    predicted,
    green,
    fraction,
    final,
    table_z,
    take_table,
    out_vel,
    out_green,
    out_frac,
    vel,
    sems,
):
    store_green = pltpu.make_async_copy(green, out_green, sems.at[0])
    store_frac = pltpu.make_async_copy(fraction, out_frac, sems.at[1])
    store_green.start()
    store_frac.start()
    taken = jnp.concatenate([take_table[...], take_table[...]], axis=1)
    slopes = narrow_dot(taken, jnp.concatenate(split_values(final[...]), axis=1), ((1,), (1,)))
    slopes = split_dot(split_values(slopes), table_z).reshape(predicted.shape)
    vel[0] = predicted[0] - slopes[0]
    vel[1] = predicted[1] - slopes[1]
    vel[2] = predicted[2] - 0.5 * (shift(slopes[2], 1, 2) - shift(slopes[2], -1, 2))
    store_vel = pltpu.make_async_copy(vel, out_vel, sems.at[2])
    store_vel.start()
    store_vel.wait()
    store_green.wait()
    store_frac.wait()


def fused_local(count_x, count_y, velocity, cauchy_green, labels):
    cells_x, cells_y, length_z = labels.shape
    devices = count_x * count_y
    rows = length_z // devices
    length_y = count_y * cells_y
    tables = spectral_tables(count_x, count_y, cells_x, cells_y, length_z)
    lanes = (cells_x + 4) * cells_y
    back = back_lanes(cells_x, cells_y)
    plane = (cells_y, length_z)
    real = functools.partial(pltpu.VMEM, dtype=jnp.float32)
    outputs = (
        jax.ShapeDtypeStruct(velocity.shape, jnp.float32),
        jax.ShapeDtypeStruct(cauchy_green.shape, jnp.float32),
        jax.ShapeDtypeStruct(labels.shape, jnp.float32),
    )
    handed = outputs + (
        jax.ShapeDtypeStruct((length_z, back), jnp.float32),
        jax.ShapeDtypeStruct(tables[0].shape, jnp.bfloat16),
        jax.ShapeDtypeStruct(tables[6].shape, jnp.bfloat16),
    )
    near = pl.BlockSpec(memory_space=pltpu.VMEM)
    far = pl.BlockSpec(memory_space=pltpu.HBM)
    scratch = [
        real(velocity.shape),
        real(cauchy_green.shape),
        pltpu.VMEM(labels.shape, jnp.int32),
        pltpu.VMEM(tables[1].shape, jnp.bfloat16),
        pltpu.VMEM(tables[2].shape, jnp.bfloat16),
        pltpu.VMEM(tables[3].shape, jnp.bfloat16),
        real(tables[4].shape),
        real(tables[5].shape[1:]),
        pltpu.VMEM(tables[7].shape, jnp.bfloat16),
        pltpu.VMEM(tables[8].shape, jnp.bfloat16),
        real((7, cells_x) + plane),
        real((7, cells_x) + plane),
        real((7, cells_x, 8, length_z)),
        real((3, 2 * cells_x, length_z)),
        real((7, 3) + plane),
        real((7, 3) + plane),
        pltpu.VMEM((3,) + plane, jnp.int32),
        pltpu.VMEM((3,) + plane, jnp.int32),
        real((3, 1) + plane),
        real((3, 1) + plane),
        real((7, cells_x, 8, length_z)),
        real((3, 2 * cells_x, length_z)),
        real((3, cells_x, 8, length_z)),
        real((6, cells_x) + plane),
        real((3, cells_x, 8, length_z)),
        real((3, 1) + plane),
        real((3, 1) + plane),
        real((3, cells_x, 8, length_z)),
        real((devices, rows + 1, lanes)),
        real((devices, rows + 1, lanes)),
        real((devices, rows, back)),
        real((devices, rows, back)),
        pltpu.SemaphoreType.DMA((12,)),
        pltpu.SemaphoreType.DMA((2, 14)),
        pltpu.SemaphoreType.DMA((2, 3)),
        pltpu.SemaphoreType.DMA((2,)),
        pltpu.SemaphoreType.DMA((2,)),
        pltpu.SemaphoreType.REGULAR((max(count_x.bit_length() - 1 - plane_bits, 1),)),
        real((7,) + plane),
    ]
    made = pl.pallas_call(
        functools.partial(step_kernel, count_x, count_y),
        out_shape=handed,
        in_specs=[far] * 12,
        out_specs=(near,) * 6,
        scratch_shapes=scratch,
        compiler_params=pltpu.CompilerParams(
            collective_id=0, has_side_effects=True, vmem_limit_bytes=32 * 1024 * 1024
        ),
        name="membrane_step",
    )(*[
        pltpu.with_memory_space_constraint(value, pltpu.HBM)
        for value in (velocity, cauchy_green, labels, *map(jnp.asarray, tables))
    ])
    return tuple(
        pl.pallas_call(
            finish_kernel,
            out_shape=outputs,
            in_specs=[near] * 6,
            out_specs=(far,) * 3,
            scratch_shapes=[real(velocity.shape), pltpu.SemaphoreType.DMA((3,))],
            compiler_params=pltpu.CompilerParams(vmem_limit_bytes=16 * 1024 * 1024),
            name="finish_step",
        )(*made)
    )


def fits_fused(count_x, count_y, shape):
    _, length_x, length_y, length_z = shape
    cells_x, cells_y = length_x // count_x, length_y // count_y
    devices = count_x * count_y
    return (
        count_y == 2
        and count_x > 2
        and count_x & (count_x - 1) == 0
        and length_z % 128 == 0
        and length_z % devices == 0
        and length_z // devices == 4
        and (cells_x + 4) * cells_y == 128
        and cells_x <= 7
        and cells_x >= 4
        and cells_y % 8 == 0
        and cells_y >= 8
        and (cells_x + 4) * length_y % 128 == 0
        and length_x * length_y <= 4096
    )


def solution(mesh):
    placed = (P(None, "gx", "gy", None), P(None, "gx", "gy", None), P("gx", "gy", None))
    count_x, count_y = mesh.shape["gx"], mesh.shape["gy"]

    def step(velocity, cauchy_green, labels):
        if fits_fused(count_x, count_y, velocity.shape):
            body = functools.partial(fused_local, count_x, count_y)
        else:
            body = local
        return jax.shard_map(
            body, mesh=mesh, in_specs=placed, out_specs=placed, check_vma=False
        )(velocity, cauchy_green, labels)

    return step
```
